256 devices in a mesh: dp: 64 (over z, y, core), section: 4 (over x).
Axes of the slice: x: 4, y: 4, z: 8, core: 2. Of those that a mesh axis runs over, the one named last changes fastest.
Arguments:
- query_hidden: bfloat16 [32768, 4096], P('dp', 'section'), may hold values from -0.5 to 0.5
- tool_hidden: bfloat16 [32768, 4096], P('dp', 'section'), may hold values from -0.5 to 0.5
- norm_gain: float32 [4096], P('section'), may hold values from 0.5 to 1.5
- positive_tool: int32 [32768], P('dp'), may hold values from 0 to 511
- hard_owner: int32 [32768, 2], P('dp'), may hold values from 0 to 63, as said below
- hard_row: int32 [32768, 2], P('dp'), may hold values from 0 to 511
- hard_valid: int32 [32768, 2], P('dp'), may hold values from 0 to 1
Outputs:
- query_grad: bfloat16 [32768, 4096], P('dp', 'section')
- tool_grad: bfloat16 [32768, 4096], P('dp', 'section')
- gain_grad: float32 [4096], P('section')
The draws below stay inside these ranges and needn't reach their ends.
Inputs may be any that keep to these rules, and one draw needn't show every extreme that they name: `hard_owner`: each dp index's valid slots name any one owner at most 32 times; two owners, the same for every dp index and drawn from the seed, are named exactly 32 times by the valid slots of every dp index.
All inputs are finite; a program needn't handle non-finite values.
Results may differ from the reference program's by a relative error of at most 0.0067.
Values may be sent and summed in bfloat16 or wider, within the bound.
A program may use at most 128 MiB of HBM per device.

```python
import math
import jax
import jax.numpy as jnp
from jax import lax

D = 4096
QD = 512
TD = 512
HARD = 2
CAP = 32
QUERIES = 32768
TOOLS = 32768
N_DP = 64


def scaled_hidden(key, count):
    keys = jax.random.split(key, 3)
    row_scale = jnp.exp(jax.random.uniform(keys[0], (count, 1), jnp.float32, 0.0, math.log(10.0)))
    col_scale = jnp.exp(jax.random.uniform(keys[1], (1, D), jnp.float32, 0.0, math.log(10.0)))
    values = jnp.clip(jax.random.normal(keys[2], (count, D), jnp.float32), -6.0, 6.0) * col_scale
    return jnp.clip(values * row_scale * 0.001, -0.5, 0.5)


def draw_query_hidden(key, part):
    return scaled_hidden(jax.random.fold_in(key, 3), QUERIES).astype(jnp.bfloat16)


def draw_tool_hidden(key, part):
    return scaled_hidden(jax.random.fold_in(key, 5), TOOLS).astype(jnp.bfloat16)


def hard_lists(key):
    keys = [jax.random.fold_in(key, 11 + number) for number in range(8)]
    slots = QD * HARD
    shape = (N_DP, slots)
    hot = jax.random.permutation(keys[0], N_DP)[:2].astype(jnp.int32)
    lower = jnp.minimum(hot[0], hot[1])
    upper = jnp.maximum(hot[0], hot[1])
    ranks = jax.vmap(lambda single: jax.random.permutation(single, slots))(jax.random.split(keys[1], N_DP)).astype(jnp.int32)
    others = jax.random.randint(keys[2], shape, 0, N_DP - 2, jnp.int32)
    others = others + (others >= lower).astype(jnp.int32)
    others = others + (others >= upper).astype(jnp.int32)
    owners = jnp.where(ranks < CAP, hot[0], jnp.where(ranks < 2 * CAP, hot[1], others))
    forced = ranks < 2 * CAP
    usable = (jax.random.randint(keys[3], shape, 0, 16, jnp.int32) > 0) | forced
    onehot = ((owners[:, :, None] == jnp.arange(N_DP, dtype=jnp.int32)[None, None, :]) & usable[:, :, None]).astype(jnp.int32)
    counted = jnp.cumsum(onehot, axis=1)
    position = jnp.sum(counted * onehot, axis=2)
    usable = usable & (position <= CAP)
    hot_rows = jax.random.randint(keys[4], (N_DP, 8), 0, TD, jnp.int32)
    coin = jax.random.randint(keys[5], shape, 0, 2, jnp.int32)
    which = jax.random.randint(keys[6], shape, 0, 8, jnp.int32)
    spread_rows = jax.random.randint(keys[7], shape, 0, TD, jnp.int32)
    rows = jnp.where(coin == 0, hot_rows[owners, which], spread_rows)
    return (owners.reshape(QUERIES, HARD), rows.reshape(QUERIES, HARD), usable.astype(jnp.int32).reshape(QUERIES, HARD))


def draw_hard_owner(key, part):
    return hard_lists(key)[0]


def draw_hard_row(key, part):
    return hard_lists(key)[1]


def draw_hard_valid(key, part):
    return hard_lists(key)[2]


def with_ends(values, stream_key, least, high):
    index_at = [jax.random.randint(jax.random.fold_in(stream_key, axis), (), 0, length) for axis, length in enumerate(values.shape)]
    longest = values.shape.index(max(values.shape))
    beside = index_at[:longest] + [(index_at[longest] + 1) % values.shape[longest]] + index_at[longest + 1:]
    return values.at[tuple(index_at)].set(least).at[tuple(beside)].set(high)


def setup_inputs(seed: int = 0) -> dict:
    key_list = jax.random.split(jax.random.key(seed), 8)
    query_hidden = draw_query_hidden(jax.random.fold_in(key_list[7], 71), 0)
    tool_hidden = draw_tool_hidden(jax.random.fold_in(key_list[7], 71), 0)
    norm_gain = jnp.clip(1.0 + 0.1 * jax.random.normal(key_list[2], (D,), jnp.float32), 0.5, 1.5)
    positive_tool = with_ends(jax.random.randint(key_list[3], (QUERIES,), 0, TD), jax.random.fold_in(key_list[3], 1), 0, TD - 1).astype(jnp.int32)
    hard_owner = draw_hard_owner(jax.random.fold_in(key_list[7], 71), 0)
    hard_row = draw_hard_row(jax.random.fold_in(key_list[7], 71), 0)
    hard_valid = draw_hard_valid(jax.random.fold_in(key_list[7], 71), 0)
    return {"query_hidden": query_hidden, "tool_hidden": tool_hidden, "norm_gain": norm_gain, "positive_tool": positive_tool, "hard_owner": hard_owner, "hard_row": hard_row, "hard_valid": hard_valid}


EPSILON = 1e-06
SOFTMAX_TEMP = 0.05

def unit_rows(hidden, gain):
    scaled = hidden.astype(jnp.float32) * gain
    norms = jnp.sqrt(lax.optimization_barrier(jnp.sum(scaled * scaled, axis=-1)) + EPSILON)
    return (scaled / norms[..., None], norms)

def softmax_grads(shard_scores, negative_scores, positive, valid_mask):
    selected_rows = lax.broadcasted_iota(jnp.int32, shard_scores.shape, 1) == positive[:, None]
    softmax_weights = jnp.exp(shard_scores / SOFTMAX_TEMP)
    shard_probabilities = softmax_weights / lax.optimization_barrier(jnp.sum(softmax_weights, axis=1, keepdims=True))
    positive_score = lax.optimization_barrier(jnp.sum(jnp.where(selected_rows, shard_scores, 0.0), axis=1))
    positive_weight = jnp.exp(positive_score / SOFTMAX_TEMP)
    negative_weights = jnp.where(valid_mask > 0, jnp.exp(negative_scores / SOFTMAX_TEMP), 0.0)
    negative_weight_sum = positive_weight + lax.optimization_barrier(jnp.sum(negative_weights, axis=1))
    shard_gradients = ((shard_probabilities + jnp.where(selected_rows, (positive_weight / negative_weight_sum - 2.0)[:, None], 0.0)) / SOFTMAX_TEMP).astype(jnp.bfloat16)
    negative_gradients = (negative_weights / (negative_weight_sum[:, None] * SOFTMAX_TEMP)).astype(jnp.bfloat16)
    return (shard_gradients, negative_gradients)

def reference(query_hidden, tool_hidden, norm_gain, positive_tool, hard_owner, hard_row, hard_valid):
    gain = norm_gain.astype(jnp.float32)
    query_blocks = query_hidden.reshape(N_DP, QD, D)
    tool_blocks = tool_hidden.reshape(N_DP, TD, D)
    tool_norm = lax.map(lambda block: unit_rows(block, gain)[1], tool_blocks).reshape(-1)
    query_norm = lax.map(lambda block: unit_rows(block, gain)[1], query_blocks).reshape(-1)
    global_ids = (hard_owner * TD + hard_row).astype(jnp.int32)

    def query_step(carry, inputs):
        hidden, tools, positive, ids, valid_mask = inputs
        query_unit32, norms = unit_rows(hidden, gain)
        query_unit = query_unit32.astype(jnp.bfloat16)
        tool_unit = unit_rows(tools, gain)[0].astype(jnp.bfloat16)
        hard_hidden = tool_hidden[ids].astype(jnp.float32)
        hard_unit = (hard_hidden * gain / tool_norm[ids][..., None]).astype(jnp.bfloat16)
        shard_scores = jnp.dot(query_unit, tool_unit.T, preferred_element_type=jnp.float32)
        negative_scores = jnp.einsum('qd,qkd->qk', query_unit.astype(jnp.float32), hard_unit.astype(jnp.float32))
        shard_gradients, negative_gradients = softmax_grads(shard_scores, negative_scores, positive, valid_mask)
        query_pull = jnp.dot(shard_gradients, tool_unit, preferred_element_type=jnp.float32)
        query_pull = query_pull + jnp.einsum('qk,qkd->qd', negative_gradients.astype(jnp.float32), hard_unit.astype(jnp.float32))
        inner = lax.optimization_barrier(jnp.sum(query_unit32 * query_pull, axis=1))
        query_back = (query_pull - query_unit32 * inner[:, None]) / norms[:, None]
        query_grad = (query_back * gain).astype(jnp.bfloat16)
        carry = carry + lax.optimization_barrier(jnp.sum(query_back * hidden.astype(jnp.float32), axis=0))
        return (carry, (query_grad, shard_gradients, negative_gradients))
    inputs = (query_blocks, tool_blocks, positive_tool.reshape(N_DP, QD), global_ids.reshape(N_DP, QD, HARD), hard_valid.reshape(N_DP, QD, HARD))
    gain_sum, (query_grads, local_all, hard_all) = lax.scan(query_step, jnp.zeros((D,), jnp.float32), inputs)
    flat_ids = jnp.where(hard_valid.reshape(-1) > 0, global_ids.reshape(-1), N_DP * TD).astype(jnp.int32)
    order = jnp.argsort(flat_ids, stable=True).astype(jnp.int32)
    sorted_ids = flat_ids[order]
    span = N_DP * CAP
    order_pad = jnp.concatenate([order, jnp.zeros((span,), jnp.int32)])
    sorted_pad = jnp.concatenate([sorted_ids, jnp.full((span,), N_DP * TD, jnp.int32)])
    starts = jnp.searchsorted(sorted_ids, jnp.arange(N_DP, dtype=jnp.int32) * TD).astype(jnp.int32)
    hard_flat = hard_all.reshape(-1)

    def tool_step(carry, inputs):
        block, hidden, queries, shard_gradients = inputs
        tool_unit32, norms = unit_rows(hidden, gain)
        query_unit = unit_rows(queries, gain)[0].astype(jnp.bfloat16)
        tool_pull = jnp.dot(shard_gradients.T, query_unit, preferred_element_type=jnp.float32)
        selected_rows = lax.dynamic_slice(order_pad, (starts[block],), (span,))
        picked_ids = lax.dynamic_slice(sorted_pad, (starts[block],), (span,))
        inside = picked_ids < (block + 1) * TD
        senders = (selected_rows // HARD).astype(jnp.int32)
        sender_unit = (query_hidden[senders].astype(jnp.float32) * gain / query_norm[senders][:, None]).astype(jnp.bfloat16)
        softmax_weights = jnp.where(inside, hard_flat[selected_rows].astype(jnp.float32), 0.0)
        terms = softmax_weights[:, None] * sender_unit.astype(jnp.float32)
        places = jnp.where(inside, picked_ids - block * TD, 0).astype(jnp.int32)
        tool_pull = tool_pull + jax.ops.segment_sum(terms, places, num_segments=TD)
        inner = lax.optimization_barrier(jnp.sum(tool_unit32 * tool_pull, axis=1))
        tool_back = (tool_pull - tool_unit32 * inner[:, None]) / norms[:, None]
        tool_grad = (tool_back * gain).astype(jnp.bfloat16)
        carry = carry + lax.optimization_barrier(jnp.sum(tool_back * hidden.astype(jnp.float32), axis=0))
        return (carry, tool_grad)
    tool_inputs = (jnp.arange(N_DP, dtype=jnp.int32), tool_blocks, query_blocks, local_all)
    gain_sum, tool_grads = lax.scan(tool_step, gain_sum, tool_inputs)
    return (query_grads.reshape(QUERIES, D), tool_grads.reshape(TOOLS, D), gain_sum)
```

```python
import jax
import jax.numpy as jnp
import numpy as np
from jax import lax
from jax.sharding import Mesh
from jax.sharding import PartitionSpec as P

EPSILON = 1e-06
SOFTMAX_TEMP = 0.05
DP = ("dz", "dy", "dc")


def softmax_grads(shard_scores, negative_scores, positive, valid_mask):
    selected_rows = lax.broadcasted_iota(jnp.int32, shard_scores.shape, 1) == positive[:, None]
    softmax_weights = jnp.exp(shard_scores / SOFTMAX_TEMP)
    shard_probabilities = softmax_weights / jnp.sum(softmax_weights, axis=1, keepdims=True)
    positive_score = jnp.sum(jnp.where(selected_rows, shard_scores, 0.0), axis=1)
    positive_weight = jnp.exp(positive_score / SOFTMAX_TEMP)
    negative_weights = jnp.where(valid_mask > 0, jnp.exp(negative_scores / SOFTMAX_TEMP), 0.0)
    negative_weight_sum = positive_weight + jnp.sum(negative_weights, axis=1)
    shard_gradients = (
        (
            shard_probabilities
            + jnp.where(selected_rows, (positive_weight / negative_weight_sum - 2.0)[:, None], 0.0)
        )
        / SOFTMAX_TEMP
    ).astype(jnp.bfloat16)
    negative_gradients = (negative_weights / (negative_weight_sum[:, None] * SOFTMAX_TEMP)).astype(
        jnp.bfloat16
    )
    return (shard_gradients, negative_gradients)


def body(query_hidden, tool_hidden, norm_gain, positive_tool, hard_owner, hard_row, hard_valid):
    query_count, features = query_hidden.shape
    tool_count = tool_hidden.shape[0]
    per_query = hard_owner.shape[1]
    slots = query_count * per_query
    group_size = lax.axis_size(DP)
    capacity = max(2, 2 * query_count * per_query // group_size)
    places = group_size * capacity

    owners = hard_owner.reshape(-1)
    wanted_rows = hard_row.reshape(-1)
    usable = hard_valid.reshape(-1) > 0
    slot_ids = jnp.arange(slots, dtype=jnp.int32)
    same_earlier = (
        (owners[:, None] == owners[None, :]) & usable[None, :] & (slot_ids[None, :] < slot_ids[:, None])
    )
    slot_place = jnp.sum(same_earlier.astype(jnp.int32), axis=1)
    target = jnp.where(usable, owners * capacity + slot_place, places)
    place_ids = jnp.arange(places, dtype=jnp.int32)
    slot_at = target[:, None] == place_ids[None, :]
    requests = jnp.sum(jnp.where(slot_at, wanted_rows[:, None], 0), axis=0).reshape(group_size, capacity)
    indices = lax.all_to_all(requests, DP, 0, 0, tiled=True).reshape(-1)

    query_scaled = query_hidden.astype(jnp.float32) * norm_gain
    tool_scaled = tool_hidden.astype(jnp.float32) * norm_gain
    query_squares, tool_squares = lax.psum(
        (jnp.sum(query_scaled * query_scaled, axis=1), jnp.sum(tool_scaled * tool_scaled, axis=1)),
        "section",
    )
    query_norm = jnp.sqrt(query_squares + EPSILON)
    tool_norm = jnp.sqrt(tool_squares + EPSILON)
    query_unit32 = query_scaled / query_norm[:, None]
    tool_unit32 = tool_scaled / tool_norm[:, None]
    query_unit = query_unit32.astype(jnp.bfloat16)
    tool_unit = tool_unit32.astype(jnp.bfloat16)

    pick_tool = (indices[:, None] == jnp.arange(tool_count, dtype=jnp.int32)[None, :]).astype(jnp.bfloat16)
    answers = jnp.dot(pick_tool, tool_unit, preferred_element_type=jnp.float32).astype(jnp.bfloat16)
    slot_of_query = slot_at.reshape(query_count, per_query, places).any(axis=1)
    pick_query = slot_of_query.T.astype(jnp.bfloat16)
    sent_queries = jnp.dot(pick_query, query_unit, preferred_element_type=jnp.float32).astype(jnp.bfloat16)
    payload = jnp.concatenate(
        [answers.reshape(group_size, capacity, features), sent_queries.reshape(group_size, capacity, features)],
        axis=1,
    )
    received = lax.all_to_all(payload, DP, 0, 0, tiled=True)
    back = received[:, :capacity].reshape(places, features)
    arrived = received[:, capacity:].reshape(places, features)

    local_part = lax.dot_general(
        query_unit, tool_unit, (((1,), (1,)), ((), ())), preferred_element_type=jnp.float32
    )
    hard_units = jnp.dot(slot_at.astype(jnp.bfloat16), back, preferred_element_type=jnp.float32).reshape(
        query_count, per_query, features
    )
    hard_part = jnp.einsum(
        "qd,qkd->qk", query_unit.astype(jnp.float32), hard_units, preferred_element_type=jnp.float32
    )
    shard_scores, negative_scores = (
        lax.psum(local_part.astype(jnp.bfloat16), "section").astype(jnp.float32),
        lax.psum(hard_part.astype(jnp.bfloat16), "section").astype(jnp.float32),
    )
    shard_gradients, negative_gradients = softmax_grads(
        shard_scores, negative_scores, positive_tool, hard_valid
    )
    query_pull = jnp.dot(shard_gradients, tool_unit, preferred_element_type=jnp.float32)
    query_pull = query_pull + jnp.einsum(
        "qk,qkd->qd", negative_gradients.astype(jnp.float32), hard_units, preferred_element_type=jnp.float32
    )

    sent_grads = jnp.sum(
        jnp.where(slot_at, negative_gradients.reshape(-1)[:, None].astype(jnp.float32), 0.0), axis=0
    ).astype(jnp.bfloat16)
    arrived_grads = lax.all_to_all(sent_grads.reshape(group_size, capacity), DP, 0, 0, tiled=True).reshape(-1)
    weights = jnp.where(
        jnp.arange(tool_count, dtype=jnp.int32)[:, None] == indices[None, :], arrived_grads[None, :], 0.0
    ).astype(jnp.bfloat16)
    tool_pull = lax.dot_general(
        shard_gradients, query_unit, (((0,), (0,)), ((), ())), preferred_element_type=jnp.float32
    )
    tool_pull = tool_pull + jnp.dot(weights, arrived, preferred_element_type=jnp.float32)

    query_inner, tool_inner = lax.psum(
        (jnp.sum(query_unit32 * query_pull, axis=1), jnp.sum(tool_unit32 * tool_pull, axis=1)),
        "section",
    )
    query_back = (query_pull - query_unit32 * query_inner[:, None]) / query_norm[:, None]
    tool_back = (tool_pull - tool_unit32 * tool_inner[:, None]) / tool_norm[:, None]
    query_grad = (query_back * norm_gain).astype(jnp.bfloat16)
    tool_grad = (tool_back * norm_gain).astype(jnp.bfloat16)
    gain_terms = jnp.sum(query_back * query_hidden.astype(jnp.float32), axis=0) + jnp.sum(
        tool_back * tool_hidden.astype(jnp.float32), axis=0
    )
    gain_grad = lax.psum(lax.psum(lax.psum(gain_terms, "dc"), "dy"), "dz")
    return (query_grad, tool_grad, gain_grad)


def split_dp(mesh):
    dp = mesh.shape["dp"]
    cores = 2 if dp % 2 == 0 else 1
    rest = dp // cores
    ys = 4 if rest % 4 == 0 else 1
    devices = np.asarray(mesh.devices).reshape(rest // ys, ys, cores, mesh.shape["section"])
    return Mesh(devices, DP + ("section",))


def solution(mesh):
    fine = split_dp(mesh)
    return jax.shard_map(
        body,
        mesh=fine,
        in_specs=(
            P(DP, "section"),
            P(DP, "section"),
            P("section"),
            P(DP),
            P(DP, None),
            P(DP, None),
            P(DP, None),
        ),
        out_specs=(P(DP, "section"), P(DP, "section"), P("section")),
        check_vma=False,
    )
```

```python
import jax
import jax.numpy as jnp
import numpy as np
from jax import lax
from jax.sharding import Mesh
from jax.sharding import PartitionSpec as P

EPSILON = 1e-06
SOFTMAX_TEMP = 0.05
DP = ("dz", "dy", "dc")


def softmax_grads(shard_scores, negative_scores, positive, valid_mask):
    selected_rows = lax.broadcasted_iota(jnp.int32, shard_scores.shape, 1) == positive[:, None]
    softmax_weights = jnp.exp(shard_scores / SOFTMAX_TEMP)
    shard_probabilities = softmax_weights / jnp.sum(softmax_weights, axis=1, keepdims=True)
    positive_score = jnp.sum(jnp.where(selected_rows, shard_scores, 0.0), axis=1)
    positive_weight = jnp.exp(positive_score / SOFTMAX_TEMP)
    negative_weights = jnp.where(valid_mask > 0, jnp.exp(negative_scores / SOFTMAX_TEMP), 0.0)
    negative_weight_sum = positive_weight + jnp.sum(negative_weights, axis=1)
    shard_gradients = (
        (
            shard_probabilities
            + jnp.where(selected_rows, (positive_weight / negative_weight_sum - 2.0)[:, None], 0.0)
        )
        / SOFTMAX_TEMP
    ).astype(jnp.bfloat16)
    negative_gradients = (negative_weights / (negative_weight_sum[:, None] * SOFTMAX_TEMP)).astype(
        jnp.bfloat16
    )
    return (shard_gradients, negative_gradients)


def body(query_hidden, tool_hidden, norm_gain, positive_tool, hard_owner, hard_row, hard_valid):
    query_count, features = query_hidden.shape
    tool_count = tool_hidden.shape[0]
    per_query = hard_owner.shape[1]
    slots = query_count * per_query
    group_size = lax.axis_size(DP)
    capacity = max(2, 2 * query_count * per_query // group_size)
    places = group_size * capacity

    owners = hard_owner.reshape(-1)
    wanted_rows = hard_row.reshape(-1)
    usable = hard_valid.reshape(-1) > 0
    slot_ids = jnp.arange(slots, dtype=jnp.int32)
    same_earlier = (
        (owners[:, None] == owners[None, :]) & usable[None, :] & (slot_ids[None, :] < slot_ids[:, None])
    )
    slot_place = jnp.sum(same_earlier.astype(jnp.int32), axis=1)
    target = jnp.where(usable, owners * capacity + slot_place, places)
    place_ids = jnp.arange(places, dtype=jnp.int32)
    slot_at = target[:, None] == place_ids[None, :]
    requests = jnp.sum(jnp.where(slot_at, wanted_rows[:, None], 0), axis=0).reshape(group_size, capacity)
    indices = lax.all_to_all(requests, DP, 0, 0, tiled=True).reshape(-1)

    query_scaled = query_hidden.astype(jnp.float32) * norm_gain
    tool_scaled = tool_hidden.astype(jnp.float32) * norm_gain
    query_squares, tool_squares = lax.psum(
        (jnp.sum(query_scaled * query_scaled, axis=1), jnp.sum(tool_scaled * tool_scaled, axis=1)),
        "section",
    )
    query_norm = jnp.sqrt(query_squares + EPSILON)
    tool_norm = jnp.sqrt(tool_squares + EPSILON)
    query_unit32 = query_scaled / query_norm[:, None]
    tool_unit32 = tool_scaled / tool_norm[:, None]
    query_unit = query_unit32.astype(jnp.bfloat16)
    tool_unit = tool_unit32.astype(jnp.bfloat16)

    slot_of_query = slot_at.reshape(query_count, per_query, places).any(axis=1)
    pick_query = slot_of_query.T.astype(jnp.bfloat16)
    sent_queries = jnp.dot(pick_query, query_unit, preferred_element_type=jnp.float32).astype(jnp.bfloat16)
    arrived_unit = lax.all_to_all(
        sent_queries.reshape(group_size, capacity, features), DP, 0, 0, tiled=True
    ).reshape(places, features)
    arrived_unit, indices, tool_picked = lax.optimization_barrier((arrived_unit, indices, tool_unit))
    tool_ids = jnp.arange(tool_count, dtype=jnp.int32)
    pick_tool = (indices[:, None] == tool_ids[None, :]).astype(jnp.bfloat16)
    answers = jnp.dot(pick_tool, tool_picked, preferred_element_type=jnp.float32).astype(jnp.bfloat16)
    back_unit = lax.all_to_all(
        answers.reshape(group_size, capacity, features), DP, 0, 0, tiled=True
    ).reshape(places, features)

    local_part = lax.dot_general(
        query_unit, tool_unit, (((1,), (1,)), ((), ())), preferred_element_type=jnp.float32
    )
    slot_grid = slot_at.reshape(query_count, per_query, places)
    every_place = lax.dot_general(
        query_unit, back_unit, (((1,), (1,)), ((), ())), preferred_element_type=jnp.float32
    )
    hard_part = jnp.sum(jnp.where(slot_grid, every_place[:, None, :], 0.0), axis=2)
    shard_scores, negative_scores = (
        lax.psum(local_part.astype(jnp.bfloat16), "section").astype(jnp.float32),
        lax.psum(hard_part.astype(jnp.bfloat16), "section").astype(jnp.float32),
    )
    shard_gradients, negative_gradients = softmax_grads(
        shard_scores, negative_scores, positive_tool, hard_valid
    )
    spread_grads = jnp.sum(
        jnp.where(slot_grid, negative_gradients.astype(jnp.float32)[:, :, None], 0.0), axis=1
    ).astype(jnp.bfloat16)
    query_pull = jnp.dot(shard_gradients, tool_unit, preferred_element_type=jnp.float32)
    query_pull = query_pull + jnp.dot(spread_grads, back_unit, preferred_element_type=jnp.float32)

    sent_grads = jnp.sum(spread_grads.astype(jnp.float32), axis=0).astype(jnp.bfloat16)
    arrived_grads = lax.all_to_all(sent_grads.reshape(group_size, capacity), DP, 0, 0, tiled=True).reshape(-1)
    weights = jnp.where(tool_ids[:, None] == indices[None, :], arrived_grads[None, :], 0.0).astype(jnp.bfloat16)
    tool_pull = lax.dot_general(
        shard_gradients, query_unit, (((0,), (0,)), ((), ())), preferred_element_type=jnp.float32
    )
    tool_pull = tool_pull + jnp.dot(weights, arrived_unit, preferred_element_type=jnp.float32)

    query_inner, tool_inner = lax.psum(
        (jnp.sum(query_unit32 * query_pull, axis=1), jnp.sum(tool_unit32 * tool_pull, axis=1)),
        "section",
    )
    query_back = (query_pull - query_unit32 * query_inner[:, None]) / query_norm[:, None]
    tool_back = (tool_pull - tool_unit32 * tool_inner[:, None]) / tool_norm[:, None]
    query_grad = (query_back * norm_gain).astype(jnp.bfloat16)
    tool_grad = (tool_back * norm_gain).astype(jnp.bfloat16)
    gain_terms = jnp.sum(query_back * query_hidden.astype(jnp.float32), axis=0) + jnp.sum(
        tool_back * tool_hidden.astype(jnp.float32), axis=0
    )
    gain_grad = lax.psum(lax.psum(lax.psum(gain_terms, "dc"), "dy"), "dz")
    return (query_grad, tool_grad, gain_grad)


def split_dp(mesh):
    dp = mesh.shape["dp"]
    cores = 2 if dp % 2 == 0 else 1
    rest = dp // cores
    ys = 4 if rest % 4 == 0 else 1
    devices = np.asarray(mesh.devices).reshape(rest // ys, ys, cores, mesh.shape["section"])
    return Mesh(devices, DP + ("section",))


def solution(mesh):
    fine = split_dp(mesh)
    return jax.shard_map(
        body,
        mesh=fine,
        in_specs=(
            P(DP, "section"),
            P(DP, "section"),
            P("section"),
            P(DP),
            P(DP, None),
            P(DP, None),
            P(DP, None),
        ),
        out_specs=(P(DP, "section"), P(DP, "section"), P("section")),
        check_vma=False,
    )
```

```python
import jax
import jax.numpy as jnp
import numpy as np
from jax import lax
from jax.sharding import Mesh
from jax.sharding import PartitionSpec as P

EPSILON = 1e-06
SOFTMAX_TEMP = 0.05
DP = ("dz", "dy", "dc")


def softmax_grads(shard_scores, negative_scores, positive, valid_mask):
    selected_rows = lax.broadcasted_iota(jnp.int32, shard_scores.shape, 1) == positive[:, None]
    softmax_weights = jnp.exp(shard_scores / SOFTMAX_TEMP)
    shard_probabilities = softmax_weights / jnp.sum(softmax_weights, axis=1, keepdims=True)
    positive_score = jnp.sum(jnp.where(selected_rows, shard_scores, 0.0), axis=1)
    positive_weight = jnp.exp(positive_score / SOFTMAX_TEMP)
    negative_weights = jnp.where(valid_mask > 0, jnp.exp(negative_scores / SOFTMAX_TEMP), 0.0)
    negative_weight_sum = positive_weight + jnp.sum(negative_weights, axis=1)
    shard_gradients = (
        (
            shard_probabilities
            + jnp.where(selected_rows, (positive_weight / negative_weight_sum - 2.0)[:, None], 0.0)
        )
        / SOFTMAX_TEMP
    ).astype(jnp.bfloat16)
    negative_gradients = (negative_weights / (negative_weight_sum[:, None] * SOFTMAX_TEMP)).astype(
        jnp.bfloat16
    )
    return (shard_gradients, negative_gradients)


def body(query_hidden, tool_hidden, norm_gain, positive_tool, hard_owner, hard_row, hard_valid):
    query_count, features = query_hidden.shape
    tool_count = tool_hidden.shape[0]
    per_query = hard_owner.shape[1]
    slots = query_count * per_query
    group_size = lax.axis_size(DP)
    capacity = max(2, 2 * query_count * per_query // group_size)
    places = group_size * capacity

    owners = hard_owner.reshape(-1)
    wanted_rows = hard_row.reshape(-1)
    usable = hard_valid.reshape(-1) > 0
    slot_ids = jnp.arange(slots, dtype=jnp.int32)
    same_earlier = (
        (owners[:, None] == owners[None, :]) & usable[None, :] & (slot_ids[None, :] < slot_ids[:, None])
    )
    slot_place = jnp.sum(same_earlier.astype(jnp.int32), axis=1)
    target = jnp.where(usable, owners * capacity + slot_place, places)
    place_ids = jnp.arange(places, dtype=jnp.int32)
    slot_at = target[:, None] == place_ids[None, :]
    requests = jnp.sum(jnp.where(slot_at, wanted_rows[:, None], 0), axis=0).reshape(group_size, capacity)
    indices = lax.all_to_all(requests, DP, 0, 0, tiled=True).reshape(-1)

    query_scaled = query_hidden.astype(jnp.float32) * norm_gain
    tool_scaled = tool_hidden.astype(jnp.float32) * norm_gain
    query_squares, tool_squares = lax.psum(
        (jnp.sum(query_scaled * query_scaled, axis=1), jnp.sum(tool_scaled * tool_scaled, axis=1)),
        "section",
    )
    query_norm = jnp.sqrt(query_squares + EPSILON)
    tool_norm = jnp.sqrt(tool_squares + EPSILON)
    query_unit32 = query_scaled / query_norm[:, None]
    tool_unit32 = tool_scaled / tool_norm[:, None]
    query_unit = query_unit32.astype(jnp.bfloat16)
    tool_unit = tool_unit32.astype(jnp.bfloat16)

    tool_ids = jnp.arange(tool_count, dtype=jnp.int32)
    pick_tool = (indices[:, None] == tool_ids[None, :]).astype(jnp.bfloat16)
    answers = jnp.dot(pick_tool, tool_unit, preferred_element_type=jnp.float32).astype(jnp.bfloat16)
    back_unit = lax.all_to_all(
        answers.reshape(group_size, capacity, features), DP, 0, 0, tiled=True
    ).reshape(places, features)

    local_part = lax.dot_general(
        query_unit, tool_unit, (((1,), (1,)), ((), ())), preferred_element_type=jnp.float32
    )
    slot_grid = slot_at.reshape(query_count, per_query, places)
    every_place = lax.dot_general(
        query_unit, back_unit, (((1,), (1,)), ((), ())), preferred_element_type=jnp.float32
    )
    hard_part = jnp.sum(jnp.where(slot_grid, every_place[:, None, :], 0.0), axis=2)
    shard_scores, negative_scores = (
        lax.psum(local_part.astype(jnp.bfloat16), "section").astype(jnp.float32),
        lax.psum(hard_part.astype(jnp.bfloat16), "section").astype(jnp.float32),
    )
    shard_gradients, negative_gradients = softmax_grads(
        shard_scores, negative_scores, positive_tool, hard_valid
    )
    spread_grads = jnp.sum(
        jnp.where(slot_grid, negative_gradients.astype(jnp.float32)[:, :, None], 0.0), axis=1
    ).astype(jnp.bfloat16)

    sent_terms = lax.dot_general(
        spread_grads, query_unit, (((0,), (0,)), ((), ())), preferred_element_type=jnp.float32
    ).astype(jnp.bfloat16)
    arrived_terms = lax.all_to_all(
        sent_terms.reshape(group_size, capacity, features), DP, 0, 0, tiled=True
    ).reshape(places, features)

    query_pull = jnp.dot(shard_gradients, tool_unit, preferred_element_type=jnp.float32)
    query_pull = query_pull + jnp.dot(spread_grads, back_unit, preferred_element_type=jnp.float32)
    tool_pull = lax.dot_general(
        shard_gradients, query_unit, (((0,), (0,)), ((), ())), preferred_element_type=jnp.float32
    )
    tool_pull = tool_pull + lax.dot_general(
        pick_tool, arrived_terms, (((0,), (0,)), ((), ())), preferred_element_type=jnp.float32
    )

    query_inner, tool_inner = lax.psum(
        (jnp.sum(query_unit32 * query_pull, axis=1), jnp.sum(tool_unit32 * tool_pull, axis=1)),
        "section",
    )
    query_back = (query_pull - query_unit32 * query_inner[:, None]) / query_norm[:, None]
    tool_back = (tool_pull - tool_unit32 * tool_inner[:, None]) / tool_norm[:, None]
    query_grad = (query_back * norm_gain).astype(jnp.bfloat16)
    tool_grad = (tool_back * norm_gain).astype(jnp.bfloat16)
    gain_terms = jnp.sum(query_back * query_hidden.astype(jnp.float32), axis=0) + jnp.sum(
        tool_back * tool_hidden.astype(jnp.float32), axis=0
    )
    gain_grad = lax.psum(lax.psum(lax.psum(gain_terms, "dc"), "dy"), "dz")
    return (query_grad, tool_grad, gain_grad)


def split_dp(mesh):
    dp = mesh.shape["dp"]
    cores = 2 if dp % 2 == 0 else 1
    rest = dp // cores
    ys = 4 if rest % 4 == 0 else 1
    devices = np.asarray(mesh.devices).reshape(rest // ys, ys, cores, mesh.shape["section"])
    return Mesh(devices, DP + ("section",))


def solution(mesh):
    fine = split_dp(mesh)
    return jax.shard_map(
        body,
        mesh=fine,
        in_specs=(
            P(DP, "section"),
            P(DP, "section"),
            P("section"),
            P(DP),
            P(DP, None),
            P(DP, None),
            P(DP, None),
        ),
        out_specs=(P(DP, "section"), P(DP, "section"), P("section")),
        check_vma=False,
    )
```

```python
import jax
import jax.numpy as jnp
import numpy as np
from jax import lax
from jax.sharding import Mesh
from jax.sharding import PartitionSpec as P

EPSILON = 1e-06
SOFTMAX_TEMP = 0.05
DP = ("dz", "dy", "dc")


def softmax_grads(shard_scores, negative_scores, positive, valid_mask):
    selected_rows = lax.broadcasted_iota(jnp.int32, shard_scores.shape, 1) == positive[:, None]
    softmax_weights = jnp.exp(shard_scores / SOFTMAX_TEMP)
    shard_probabilities = softmax_weights / jnp.sum(softmax_weights, axis=1, keepdims=True)
    positive_score = jnp.sum(jnp.where(selected_rows, shard_scores, 0.0), axis=1)
    positive_weight = jnp.exp(positive_score / SOFTMAX_TEMP)
    negative_weights = jnp.where(valid_mask > 0, jnp.exp(negative_scores / SOFTMAX_TEMP), 0.0)
    negative_weight_sum = positive_weight + jnp.sum(negative_weights, axis=1)
    shard_gradients = (
        (
            shard_probabilities
            + jnp.where(selected_rows, (positive_weight / negative_weight_sum - 2.0)[:, None], 0.0)
        )
        / SOFTMAX_TEMP
    ).astype(jnp.bfloat16)
    negative_gradients = (negative_weights / (negative_weight_sum[:, None] * SOFTMAX_TEMP)).astype(
        jnp.bfloat16
    )
    return (shard_gradients, negative_gradients)


def body(query_hidden, tool_hidden, norm_gain, positive_tool, hard_owner, hard_row, hard_valid):
    query_count, features = query_hidden.shape
    tool_count = tool_hidden.shape[0]
    per_query = hard_owner.shape[1]
    slots = query_count * per_query
    group_size = lax.axis_size(DP)
    capacity = max(2, 2 * query_count * per_query // group_size)
    places = group_size * capacity

    owners = hard_owner.reshape(-1)
    wanted_rows = hard_row.reshape(-1)
    usable = hard_valid.reshape(-1) > 0
    slot_ids = jnp.arange(slots, dtype=jnp.int32)
    same_earlier = (
        (owners[:, None] == owners[None, :]) & usable[None, :] & (slot_ids[None, :] < slot_ids[:, None])
    )
    slot_place = jnp.sum(same_earlier.astype(jnp.int32), axis=1)
    target = jnp.where(usable, owners * capacity + slot_place, places)
    place_ids = jnp.arange(places, dtype=jnp.int32)
    slot_at = target[:, None] == place_ids[None, :]
    requests = jnp.sum(jnp.where(slot_at, wanted_rows[:, None], 0), axis=0).reshape(group_size, capacity)
    indices = lax.all_to_all(requests, DP, 0, 0, tiled=True).reshape(-1)

    tool_ids = jnp.arange(tool_count, dtype=jnp.int32)
    pick_tool = (indices[:, None] == tool_ids[None, :]).astype(jnp.bfloat16)
    answers = jnp.dot(pick_tool, tool_hidden, preferred_element_type=jnp.float32).astype(jnp.bfloat16)
    back_hidden = lax.all_to_all(
        answers.reshape(group_size, capacity, features), DP, 0, 0, tiled=True
    ).reshape(places, features)

    query_scaled = query_hidden.astype(jnp.float32) * norm_gain
    tool_scaled = tool_hidden.astype(jnp.float32) * norm_gain
    query_squares, tool_squares = lax.psum(
        (jnp.sum(query_scaled * query_scaled, axis=1), jnp.sum(tool_scaled * tool_scaled, axis=1)),
        "section",
    )
    query_norm = jnp.sqrt(query_squares + EPSILON)
    tool_norm = jnp.sqrt(tool_squares + EPSILON)
    query_unit32 = query_scaled / query_norm[:, None]
    tool_unit32 = tool_scaled / tool_norm[:, None]
    query_unit = query_unit32.astype(jnp.bfloat16)
    tool_unit = tool_unit32.astype(jnp.bfloat16)

    local_part = lax.dot_general(
        query_unit, tool_unit, (((1,), (1,)), ((), ())), preferred_element_type=jnp.float32
    )
    shard_scores = lax.psum(local_part.astype(jnp.bfloat16), "section").astype(jnp.float32)
    back_hidden, query_unit, shard_scores = lax.optimization_barrier((back_hidden, query_unit, shard_scores))

    back_scaled = back_hidden.astype(jnp.float32) * norm_gain
    slot_grid = slot_at.reshape(query_count, per_query, places)
    every_place = lax.dot_general(
        query_unit, back_scaled.astype(jnp.bfloat16), (((1,), (1,)), ((), ())),
        preferred_element_type=jnp.float32,
    )
    hard_dot = jnp.sum(jnp.where(slot_grid, every_place[:, None, :], 0.0), axis=2)
    summed = lax.psum(
        jnp.concatenate([jnp.sum(back_scaled * back_scaled, axis=1), hard_dot.reshape(-1)]), "section"
    )
    back_squares, hard_dot = summed[:places], summed[places:].reshape(query_count, per_query)
    back_norm = jnp.sqrt(back_squares + EPSILON)
    back_unit = (back_scaled / back_norm[:, None]).astype(jnp.bfloat16)
    slot_norm = jnp.sum(jnp.where(slot_grid, back_norm[None, None, :], 0.0), axis=2)
    negative_scores = hard_dot / jnp.where(hard_valid > 0, slot_norm, 1.0)
    shard_gradients, negative_gradients = softmax_grads(
        shard_scores, negative_scores, positive_tool, hard_valid
    )
    spread_grads = jnp.sum(
        jnp.where(slot_grid, negative_gradients.astype(jnp.float32)[:, :, None], 0.0), axis=1
    ).astype(jnp.bfloat16)

    sent_terms = lax.dot_general(
        spread_grads, query_unit, (((0,), (0,)), ((), ())), preferred_element_type=jnp.float32
    ).astype(jnp.bfloat16)
    arrived_terms = lax.all_to_all(
        sent_terms.reshape(group_size, capacity, features), DP, 0, 0, tiled=True
    ).reshape(places, features)

    query_pull = jnp.dot(shard_gradients, tool_unit, preferred_element_type=jnp.float32)
    query_pull = query_pull + jnp.dot(spread_grads, back_unit, preferred_element_type=jnp.float32)
    tool_pull = lax.dot_general(
        shard_gradients, query_unit, (((0,), (0,)), ((), ())), preferred_element_type=jnp.float32
    )
    tool_pull = tool_pull + lax.dot_general(
        pick_tool, arrived_terms, (((0,), (0,)), ((), ())), preferred_element_type=jnp.float32
    )

    query_inner, tool_inner = lax.psum(
        (jnp.sum(query_unit32 * query_pull, axis=1), jnp.sum(tool_unit32 * tool_pull, axis=1)),
        "section",
    )
    query_back = (query_pull - query_unit32 * query_inner[:, None]) / query_norm[:, None]
    tool_back = (tool_pull - tool_unit32 * tool_inner[:, None]) / tool_norm[:, None]
    query_grad = (query_back * norm_gain).astype(jnp.bfloat16)
    tool_grad = (tool_back * norm_gain).astype(jnp.bfloat16)
    gain_terms = jnp.sum(query_back * query_hidden.astype(jnp.float32), axis=0) + jnp.sum(
        tool_back * tool_hidden.astype(jnp.float32), axis=0
    )
    chunks = gain_terms.reshape(group_size, -1)
    owned = jnp.sum(lax.all_to_all(chunks, DP, 0, 0, tiled=True), axis=0)
    gain_grad = lax.all_to_all(
        jnp.broadcast_to(owned[None, :], chunks.shape), DP, 0, 0, tiled=True
    ).reshape(-1)
    return (query_grad, tool_grad, gain_grad)


def split_dp(mesh):
    dp = mesh.shape["dp"]
    cores = 2 if dp % 2 == 0 else 1
    rest = dp // cores
    ys = 4 if rest % 4 == 0 else 1
    devices = np.asarray(mesh.devices).reshape(rest // ys, ys, cores, mesh.shape["section"])
    return Mesh(devices, DP + ("section",))


def solution(mesh):
    fine = split_dp(mesh)
    return jax.shard_map(
        body,
        mesh=fine,
        in_specs=(
            P(DP, "section"),
            P(DP, "section"),
            P("section"),
            P(DP),
            P(DP, None),
            P(DP, None),
            P(DP, None),
        ),
        out_specs=(P(DP, "section"), P(DP, "section"), P("section")),
        check_vma=False,
    )
```

```python
import jax
import jax.numpy as jnp
import numpy as np
from jax import lax
from jax.sharding import Mesh
from jax.sharding import PartitionSpec as P

EPSILON = 1e-06
SOFTMAX_TEMP = 0.05
DP = ("dz", "dy", "dc")


def softmax_grads(shard_scores, negative_scores, positive, valid_mask):
    selected_rows = lax.broadcasted_iota(jnp.int32, shard_scores.shape, 1) == positive[:, None]
    softmax_weights = jnp.exp(shard_scores / SOFTMAX_TEMP)
    shard_probabilities = softmax_weights / jnp.sum(softmax_weights, axis=1, keepdims=True)
    positive_score = jnp.sum(jnp.where(selected_rows, shard_scores, 0.0), axis=1)
    positive_weight = jnp.exp(positive_score / SOFTMAX_TEMP)
    negative_weights = jnp.where(valid_mask > 0, jnp.exp(negative_scores / SOFTMAX_TEMP), 0.0)
    negative_weight_sum = positive_weight + jnp.sum(negative_weights, axis=1)
    shard_gradients = (
        (
            shard_probabilities
            + jnp.where(selected_rows, (positive_weight / negative_weight_sum - 2.0)[:, None], 0.0)
        )
        / SOFTMAX_TEMP
    ).astype(jnp.bfloat16)
    negative_gradients = (negative_weights / (negative_weight_sum[:, None] * SOFTMAX_TEMP)).astype(
        jnp.bfloat16
    )
    return (shard_gradients, negative_gradients)


def body(query_hidden, tool_hidden, norm_gain, positive_tool, hard_owner, hard_row, hard_valid):
    query_count, features = query_hidden.shape
    tool_count = tool_hidden.shape[0]
    per_query = hard_owner.shape[1]
    slots = query_count * per_query
    group_size = lax.axis_size(DP)
    capacity = max(2, 2 * query_count * per_query // group_size)
    places = group_size * capacity

    owners = hard_owner.reshape(-1)
    wanted_rows = hard_row.reshape(-1)
    usable = hard_valid.reshape(-1) > 0
    slot_ids = jnp.arange(slots, dtype=jnp.int32)
    same_earlier = (
        (owners[:, None] == owners[None, :]) & usable[None, :] & (slot_ids[None, :] < slot_ids[:, None])
    )
    slot_place = jnp.sum(same_earlier.astype(jnp.int32), axis=1)
    target = jnp.where(usable, owners * capacity + slot_place, places)
    place_ids = jnp.arange(places, dtype=jnp.int32)
    slot_at = target[:, None] == place_ids[None, :]
    requests = jnp.sum(jnp.where(slot_at, wanted_rows[:, None], 0), axis=0).reshape(group_size, capacity)
    indices = lax.all_to_all(requests, DP, 0, 0, tiled=True).reshape(-1)

    query_scaled = query_hidden.astype(jnp.float32) * norm_gain
    tool_scaled = tool_hidden.astype(jnp.float32) * norm_gain
    query_squares, tool_squares = lax.psum(
        (jnp.sum(query_scaled * query_scaled, axis=1), jnp.sum(tool_scaled * tool_scaled, axis=1)),
        "section",
    )
    query_norm = jnp.sqrt(query_squares + EPSILON)
    tool_norm = jnp.sqrt(tool_squares + EPSILON)
    query_unit32 = query_scaled / query_norm[:, None]
    tool_unit32 = tool_scaled / tool_norm[:, None]
    query_unit = query_unit32.astype(jnp.bfloat16)
    tool_unit = tool_unit32.astype(jnp.bfloat16)

    tool_ids = jnp.arange(tool_count, dtype=jnp.int32)
    pick_tool = (indices[:, None] == tool_ids[None, :]).astype(jnp.bfloat16)
    answers = jnp.dot(pick_tool, tool_unit, preferred_element_type=jnp.float32).astype(jnp.bfloat16)
    back_unit = lax.all_to_all(
        answers.reshape(group_size, capacity, features), DP, 0, 0, tiled=True
    ).reshape(places, features)

    local_part = lax.dot_general(
        query_unit, tool_unit, (((1,), (1,)), ((), ())), preferred_element_type=jnp.float32
    )
    slot_grid = slot_at.reshape(query_count, per_query, places)
    every_place = lax.dot_general(
        query_unit, back_unit, (((1,), (1,)), ((), ())), preferred_element_type=jnp.float32
    )
    hard_part = jnp.sum(jnp.where(slot_grid, every_place[:, None, :], 0.0), axis=2)
    shard_scores, negative_scores = (
        lax.psum(local_part.astype(jnp.bfloat16), "section").astype(jnp.float32),
        lax.psum(hard_part.astype(jnp.bfloat16), "section").astype(jnp.float32),
    )
    shard_gradients, negative_gradients = softmax_grads(
        shard_scores, negative_scores, positive_tool, hard_valid
    )
    spread_grads = jnp.sum(
        jnp.where(slot_grid, negative_gradients.astype(jnp.float32)[:, :, None], 0.0), axis=1
    ).astype(jnp.bfloat16)

    sent_terms = lax.dot_general(
        spread_grads, query_unit, (((0,), (0,)), ((), ())), preferred_element_type=jnp.float32
    ).astype(jnp.bfloat16)
    arrived_terms = lax.all_to_all(
        sent_terms.reshape(group_size, capacity, features), DP, 0, 0, tiled=True
    ).reshape(places, features)

    query_pull = jnp.dot(shard_gradients, tool_unit, preferred_element_type=jnp.float32)
    query_pull = query_pull + jnp.dot(spread_grads, back_unit, preferred_element_type=jnp.float32)
    tool_pull = lax.dot_general(
        shard_gradients, query_unit, (((0,), (0,)), ((), ())), preferred_element_type=jnp.float32
    )
    tool_pull = tool_pull + lax.dot_general(
        pick_tool, arrived_terms, (((0,), (0,)), ((), ())), preferred_element_type=jnp.float32
    )

    query_inner, tool_inner = lax.psum(
        (jnp.sum(query_unit32 * query_pull, axis=1), jnp.sum(tool_unit32 * tool_pull, axis=1)),
        "section",
    )
    query_back = (query_pull - query_unit32 * query_inner[:, None]) / query_norm[:, None]
    tool_back = (tool_pull - tool_unit32 * tool_inner[:, None]) / tool_norm[:, None]
    query_grad = (query_back * norm_gain).astype(jnp.bfloat16)
    tool_grad = (tool_back * norm_gain).astype(jnp.bfloat16)
    gain_terms = jnp.sum(query_back * query_hidden.astype(jnp.float32), axis=0) + jnp.sum(
        tool_back * tool_hidden.astype(jnp.float32), axis=0
    )
    everyone = jnp.broadcast_to(gain_terms[None, :], (group_size, gain_terms.shape[0]))
    gain_grad = jnp.sum(lax.all_to_all(everyone, DP, 0, 0, tiled=True), axis=0)
    return (query_grad, tool_grad, gain_grad)


def split_dp(mesh):
    dp = mesh.shape["dp"]
    cores = 2 if dp % 2 == 0 else 1
    rest = dp // cores
    ys = 4 if rest % 4 == 0 else 1
    devices = np.asarray(mesh.devices).reshape(rest // ys, ys, cores, mesh.shape["section"])
    return Mesh(devices, DP + ("section",))


def solution(mesh):
    fine = split_dp(mesh)
    return jax.shard_map(
        body,
        mesh=fine,
        in_specs=(
            P(DP, "section"),
            P(DP, "section"),
            P("section"),
            P(DP),
            P(DP, None),
            P(DP, None),
            P(DP, None),
        ),
        out_specs=(P(DP, "section"), P(DP, "section"), P("section")),
        check_vma=False,
    )
```

```python
import jax
import jax.numpy as jnp
import numpy as np
from jax import lax
from jax.sharding import Mesh
from jax.sharding import PartitionSpec as P

EPSILON = 1e-06
SOFTMAX_TEMP = 0.05
DP = ("dz", "dy", "dc")


def softmax_grads(shard_scores, negative_scores, positive, valid_mask):
    selected_rows = lax.broadcasted_iota(jnp.int32, shard_scores.shape, 1) == positive[:, None]
    softmax_weights = jnp.exp(shard_scores / SOFTMAX_TEMP)
    shard_probabilities = softmax_weights / jnp.sum(softmax_weights, axis=1, keepdims=True)
    positive_score = jnp.sum(jnp.where(selected_rows, shard_scores, 0.0), axis=1)
    positive_weight = jnp.exp(positive_score / SOFTMAX_TEMP)
    negative_weights = jnp.where(valid_mask > 0, jnp.exp(negative_scores / SOFTMAX_TEMP), 0.0)
    negative_weight_sum = positive_weight + jnp.sum(negative_weights, axis=1)
    shard_gradients = (
        (
            shard_probabilities
            + jnp.where(selected_rows, (positive_weight / negative_weight_sum - 2.0)[:, None], 0.0)
        )
        / SOFTMAX_TEMP
    ).astype(jnp.bfloat16)
    negative_gradients = (negative_weights / (negative_weight_sum[:, None] * SOFTMAX_TEMP)).astype(
        jnp.bfloat16
    )
    return (shard_gradients, negative_gradients)


def section_sum(value):
    parts = lax.axis_size("section")
    flat = value.reshape(-1)
    gathered = lax.all_to_all(jnp.broadcast_to(flat[None, :], (parts, flat.shape[0])), "section", 0, 0, tiled=True)
    return jnp.sum(gathered.astype(jnp.float32), axis=0).reshape(value.shape)


def body(query_hidden, tool_hidden, norm_gain, positive_tool, hard_owner, hard_row, hard_valid):
    query_count, features = query_hidden.shape
    tool_count = tool_hidden.shape[0]
    per_query = hard_owner.shape[1]
    slots = query_count * per_query
    group_size = lax.axis_size(DP)
    capacity = max(2, 2 * query_count * per_query // group_size)
    places = group_size * capacity

    owners = hard_owner.reshape(-1)
    wanted_rows = hard_row.reshape(-1)
    usable = hard_valid.reshape(-1) > 0
    slot_ids = jnp.arange(slots, dtype=jnp.int32)
    same_earlier = (
        (owners[:, None] == owners[None, :]) & usable[None, :] & (slot_ids[None, :] < slot_ids[:, None])
    )
    slot_place = jnp.sum(same_earlier.astype(jnp.int32), axis=1)
    target = jnp.where(usable, owners * capacity + slot_place, places)
    place_ids = jnp.arange(places, dtype=jnp.int32)
    slot_at = target[:, None] == place_ids[None, :]
    requests = jnp.sum(jnp.where(slot_at, wanted_rows[:, None], 0), axis=0).reshape(group_size, capacity)
    indices = lax.all_to_all(requests, DP, 0, 0, tiled=True).reshape(-1)

    query_scaled = query_hidden.astype(jnp.float32) * norm_gain
    tool_scaled = tool_hidden.astype(jnp.float32) * norm_gain
    squares = section_sum(
        jnp.stack([jnp.sum(query_scaled * query_scaled, axis=1), jnp.sum(tool_scaled * tool_scaled, axis=1)])
    )
    query_squares, tool_squares = squares[0], squares[1]
    query_norm = jnp.sqrt(query_squares + EPSILON)
    tool_norm = jnp.sqrt(tool_squares + EPSILON)
    query_unit32 = query_scaled / query_norm[:, None]
    tool_unit32 = tool_scaled / tool_norm[:, None]
    query_unit = query_unit32.astype(jnp.bfloat16)
    tool_unit = tool_unit32.astype(jnp.bfloat16)

    tool_ids = jnp.arange(tool_count, dtype=jnp.int32)
    pick_tool = (indices[:, None] == tool_ids[None, :]).astype(jnp.bfloat16)
    answers = jnp.dot(pick_tool, tool_unit, preferred_element_type=jnp.float32).astype(jnp.bfloat16)
    back_unit = lax.all_to_all(
        answers.reshape(group_size, capacity, features), DP, 0, 0, tiled=True
    ).reshape(places, features)

    local_part = lax.dot_general(
        query_unit, tool_unit, (((1,), (1,)), ((), ())), preferred_element_type=jnp.float32
    )
    slot_grid = slot_at.reshape(query_count, per_query, places)
    every_place = lax.dot_general(
        query_unit, back_unit, (((1,), (1,)), ((), ())), preferred_element_type=jnp.float32
    )
    hard_part = jnp.sum(jnp.where(slot_grid, every_place[:, None, :], 0.0), axis=2)
    shard_scores, negative_scores = (
        lax.psum(local_part.astype(jnp.bfloat16), "section").astype(jnp.float32),
        section_sum(hard_part.astype(jnp.bfloat16)),
    )
    shard_gradients, negative_gradients = softmax_grads(
        shard_scores, negative_scores, positive_tool, hard_valid
    )
    spread_grads = jnp.sum(
        jnp.where(slot_grid, negative_gradients.astype(jnp.float32)[:, :, None], 0.0), axis=1
    ).astype(jnp.bfloat16)

    sent_terms = lax.dot_general(
        spread_grads, query_unit, (((0,), (0,)), ((), ())), preferred_element_type=jnp.float32
    ).astype(jnp.bfloat16)
    arrived_terms = lax.all_to_all(
        sent_terms.reshape(group_size, capacity, features), DP, 0, 0, tiled=True
    ).reshape(places, features)

    query_pull = jnp.dot(shard_gradients, tool_unit, preferred_element_type=jnp.float32)
    query_pull = query_pull + jnp.dot(spread_grads, back_unit, preferred_element_type=jnp.float32)
    tool_pull = lax.dot_general(
        shard_gradients, query_unit, (((0,), (0,)), ((), ())), preferred_element_type=jnp.float32
    )
    tool_pull = tool_pull + lax.dot_general(
        pick_tool, arrived_terms, (((0,), (0,)), ((), ())), preferred_element_type=jnp.float32
    )

    inner = section_sum(
        jnp.stack([jnp.sum(query_unit32 * query_pull, axis=1), jnp.sum(tool_unit32 * tool_pull, axis=1)])
    )
    query_inner, tool_inner = inner[0], inner[1]
    query_back = (query_pull - query_unit32 * query_inner[:, None]) / query_norm[:, None]
    tool_back = (tool_pull - tool_unit32 * tool_inner[:, None]) / tool_norm[:, None]
    query_grad = (query_back * norm_gain).astype(jnp.bfloat16)
    tool_grad = (tool_back * norm_gain).astype(jnp.bfloat16)
    gain_terms = jnp.sum(query_back * query_hidden.astype(jnp.float32), axis=0) + jnp.sum(
        tool_back * tool_hidden.astype(jnp.float32), axis=0
    )
    everyone = jnp.broadcast_to(gain_terms[None, :], (group_size, gain_terms.shape[0]))
    gain_grad = jnp.sum(lax.all_to_all(everyone, DP, 0, 0, tiled=True), axis=0)
    return (query_grad, tool_grad, gain_grad)


def split_dp(mesh):
    dp = mesh.shape["dp"]
    cores = 2 if dp % 2 == 0 else 1
    rest = dp // cores
    ys = 4 if rest % 4 == 0 else 1
    devices = np.asarray(mesh.devices).reshape(rest // ys, ys, cores, mesh.shape["section"])
    return Mesh(devices, DP + ("section",))


def solution(mesh):
    fine = split_dp(mesh)
    return jax.shard_map(
        body,
        mesh=fine,
        in_specs=(
            P(DP, "section"),
            P(DP, "section"),
            P("section"),
            P(DP),
            P(DP, None),
            P(DP, None),
            P(DP, None),
        ),
        out_specs=(P(DP, "section"), P(DP, "section"), P("section")),
        check_vma=False,
    )
```

```python
import jax
import jax.numpy as jnp
import numpy as np
from jax import lax
from jax.sharding import Mesh
from jax.sharding import PartitionSpec as P

EPSILON = 1e-06
SOFTMAX_TEMP = 0.05
DP = ("dz", "dy", "dc")


def softmax_grads(shard_scores, negative_scores, positive, valid_mask):
    selected_rows = lax.broadcasted_iota(jnp.int32, shard_scores.shape, 1) == positive[:, None]
    softmax_weights = jnp.exp(shard_scores / SOFTMAX_TEMP)
    shard_probabilities = softmax_weights / jnp.sum(softmax_weights, axis=1, keepdims=True)
    positive_score = jnp.sum(jnp.where(selected_rows, shard_scores, 0.0), axis=1)
    positive_weight = jnp.exp(positive_score / SOFTMAX_TEMP)
    negative_weights = jnp.where(valid_mask > 0, jnp.exp(negative_scores / SOFTMAX_TEMP), 0.0)
    negative_weight_sum = positive_weight + jnp.sum(negative_weights, axis=1)
    shard_gradients = (
        (
            shard_probabilities
            + jnp.where(selected_rows, (positive_weight / negative_weight_sum - 2.0)[:, None], 0.0)
        )
        / SOFTMAX_TEMP
    ).astype(jnp.bfloat16)
    negative_gradients = (negative_weights / (negative_weight_sum[:, None] * SOFTMAX_TEMP)).astype(
        jnp.bfloat16
    )
    return (shard_gradients, negative_gradients)


def section_sum(value):
    parts = lax.axis_size("section")
    flat = value.reshape(-1)
    gathered = lax.all_to_all(jnp.broadcast_to(flat[None, :], (parts, flat.shape[0])), "section", 0, 0, tiled=True)
    return jnp.sum(gathered.astype(jnp.float32), axis=0).reshape(value.shape)


def body(query_hidden, tool_hidden, norm_gain, positive_tool, hard_owner, hard_row, hard_valid):
    query_count, features = query_hidden.shape
    tool_count = tool_hidden.shape[0]
    per_query = hard_owner.shape[1]
    slots = query_count * per_query
    group_size = lax.axis_size(DP)
    capacity = max(2, 2 * query_count * per_query // group_size)
    places = group_size * capacity

    owners = hard_owner.reshape(-1)
    wanted_rows = hard_row.reshape(-1)
    usable = hard_valid.reshape(-1) > 0
    slot_ids = jnp.arange(slots, dtype=jnp.int32)
    same_earlier = (
        (owners[:, None] == owners[None, :]) & usable[None, :] & (slot_ids[None, :] < slot_ids[:, None])
    )
    slot_place = jnp.sum(same_earlier.astype(jnp.int32), axis=1)
    target = jnp.where(usable, owners * capacity + slot_place, places)
    place_ids = jnp.arange(places, dtype=jnp.int32)
    slot_at = target[:, None] == place_ids[None, :]
    requests = jnp.sum(jnp.where(slot_at, wanted_rows[:, None], 0), axis=0).reshape(group_size, capacity)
    indices = lax.all_to_all(requests, DP, 0, 0, tiled=True).reshape(-1)

    query_scaled = query_hidden.astype(jnp.float32) * norm_gain
    tool_scaled = tool_hidden.astype(jnp.float32) * norm_gain
    query_squares, tool_squares = lax.psum(
        (jnp.sum(query_scaled * query_scaled, axis=1), jnp.sum(tool_scaled * tool_scaled, axis=1)),
        "section",
    )
    query_norm = jnp.sqrt(query_squares + EPSILON)
    tool_norm = jnp.sqrt(tool_squares + EPSILON)
    query_unit32 = query_scaled / query_norm[:, None]
    tool_unit32 = tool_scaled / tool_norm[:, None]
    query_unit = query_unit32.astype(jnp.bfloat16)
    tool_unit = tool_unit32.astype(jnp.bfloat16)

    tool_ids = jnp.arange(tool_count, dtype=jnp.int32)
    pick_tool = (indices[:, None] == tool_ids[None, :]).astype(jnp.bfloat16)
    answers = jnp.dot(pick_tool, tool_unit, preferred_element_type=jnp.float32).astype(jnp.bfloat16)
    back_unit = lax.all_to_all(
        answers.reshape(group_size, capacity, features), DP, 0, 0, tiled=True
    ).reshape(places, features)

    slot_of_query = slot_at.reshape(query_count, per_query, places).any(axis=1)
    placed_queries = lax.dot_general(
        slot_of_query.astype(jnp.bfloat16), query_unit, (((0,), (0,)), ((), ())),
        preferred_element_type=jnp.float32,
    ).astype(jnp.bfloat16)
    back_unit, placed_queries = lax.optimization_barrier((back_unit, placed_queries))
    local_part = lax.dot_general(
        query_unit, tool_unit, (((1,), (1,)), ((), ())), preferred_element_type=jnp.float32
    )
    slot_grid = slot_at.reshape(query_count, per_query, places)
    every_place = lax.dot_general(
        query_unit, back_unit, (((1,), (1,)), ((), ())), preferred_element_type=jnp.float32
    )
    hard_part = jnp.sum(jnp.where(slot_grid, every_place[:, None, :], 0.0), axis=2)
    shard_scores, negative_scores = (
        lax.psum(local_part.astype(jnp.bfloat16), "section").astype(jnp.float32),
        section_sum(hard_part.astype(jnp.bfloat16)),
    )
    shard_gradients, negative_gradients = softmax_grads(
        shard_scores, negative_scores, positive_tool, hard_valid
    )
    spread_grads = jnp.sum(
        jnp.where(slot_grid, negative_gradients.astype(jnp.float32)[:, :, None], 0.0), axis=1
    ).astype(jnp.bfloat16)

    place_grads = jnp.sum(spread_grads.astype(jnp.float32), axis=0)
    sent_terms = (place_grads[:, None] * placed_queries.astype(jnp.float32)).astype(jnp.bfloat16)
    arrived_terms = lax.all_to_all(
        sent_terms.reshape(group_size, capacity, features), DP, 0, 0, tiled=True
    ).reshape(places, features)

    query_pull = jnp.dot(shard_gradients, tool_unit, preferred_element_type=jnp.float32)
    query_pull = query_pull + jnp.dot(spread_grads, back_unit, preferred_element_type=jnp.float32)
    tool_pull = lax.dot_general(
        shard_gradients, query_unit, (((0,), (0,)), ((), ())), preferred_element_type=jnp.float32
    )
    tool_pull = tool_pull + lax.dot_general(
        pick_tool, arrived_terms, (((0,), (0,)), ((), ())), preferred_element_type=jnp.float32
    )

    inner = section_sum(
        jnp.stack([jnp.sum(query_unit32 * query_pull, axis=1), jnp.sum(tool_unit32 * tool_pull, axis=1)])
    )
    query_inner, tool_inner = inner[0], inner[1]
    query_back = (query_pull - query_unit32 * query_inner[:, None]) / query_norm[:, None]
    tool_back = (tool_pull - tool_unit32 * tool_inner[:, None]) / tool_norm[:, None]
    query_grad = (query_back * norm_gain).astype(jnp.bfloat16)
    tool_grad = (tool_back * norm_gain).astype(jnp.bfloat16)
    gain_terms = jnp.sum(query_back * query_hidden.astype(jnp.float32), axis=0) + jnp.sum(
        tool_back * tool_hidden.astype(jnp.float32), axis=0
    )
    everyone = jnp.broadcast_to(gain_terms[None, :], (group_size, gain_terms.shape[0]))
    gain_grad = jnp.sum(lax.all_to_all(everyone, DP, 0, 0, tiled=True), axis=0)
    return (query_grad, tool_grad, gain_grad)


def split_dp(mesh):
    dp = mesh.shape["dp"]
    cores = 2 if dp % 2 == 0 else 1
    rest = dp // cores
    ys = 4 if rest % 4 == 0 else 1
    devices = np.asarray(mesh.devices).reshape(rest // ys, ys, cores, mesh.shape["section"])
    return Mesh(devices, DP + ("section",))


def solution(mesh):
    fine = split_dp(mesh)
    return jax.shard_map(
        body,
        mesh=fine,
        in_specs=(
            P(DP, "section"),
            P(DP, "section"),
            P("section"),
            P(DP),
            P(DP, None),
            P(DP, None),
            P(DP, None),
        ),
        out_specs=(P(DP, "section"), P(DP, "section"), P("section")),
        check_vma=False,
    )
```

```python
import jax
import jax.numpy as jnp
import numpy as np
from jax import lax
from jax.sharding import Mesh
from jax.sharding import PartitionSpec as P

EPSILON = 1e-06
SOFTMAX_TEMP = 0.05
DP = ("dz", "dy", "dc")


def softmax_grads(shard_scores, negative_scores, positive, valid_mask):
    selected_rows = lax.broadcasted_iota(jnp.int32, shard_scores.shape, 1) == positive[:, None]
    softmax_weights = jnp.exp(shard_scores / SOFTMAX_TEMP)
    shard_probabilities = softmax_weights / jnp.sum(softmax_weights, axis=1, keepdims=True)
    positive_score = jnp.sum(jnp.where(selected_rows, shard_scores, 0.0), axis=1)
    positive_weight = jnp.exp(positive_score / SOFTMAX_TEMP)
    negative_weights = jnp.where(valid_mask > 0, jnp.exp(negative_scores / SOFTMAX_TEMP), 0.0)
    negative_weight_sum = positive_weight + jnp.sum(negative_weights, axis=1)
    shard_gradients = (
        (
            shard_probabilities
            + jnp.where(selected_rows, (positive_weight / negative_weight_sum - 2.0)[:, None], 0.0)
        )
        / SOFTMAX_TEMP
    ).astype(jnp.bfloat16)
    negative_gradients = (negative_weights / (negative_weight_sum[:, None] * SOFTMAX_TEMP)).astype(
        jnp.bfloat16
    )
    return (shard_gradients, negative_gradients)


def body(query_hidden, tool_hidden, norm_gain, positive_tool, hard_owner, hard_row, hard_valid):
    query_count, features = query_hidden.shape
    tool_count = tool_hidden.shape[0]
    per_query = hard_owner.shape[1]
    slots = query_count * per_query
    group_size = lax.axis_size(DP)
    capacity = max(2, 2 * query_count * per_query // group_size)
    places = group_size * capacity

    owners = hard_owner.reshape(-1)
    wanted_rows = hard_row.reshape(-1)
    usable = hard_valid.reshape(-1) > 0
    slot_ids = jnp.arange(slots, dtype=jnp.int32)
    same_earlier = (
        (owners[:, None] == owners[None, :]) & usable[None, :] & (slot_ids[None, :] < slot_ids[:, None])
    )
    slot_place = jnp.sum(same_earlier.astype(jnp.int32), axis=1)
    target = jnp.where(usable, owners * capacity + slot_place, places)
    place_ids = jnp.arange(places, dtype=jnp.int32)
    slot_at = target[:, None] == place_ids[None, :]
    requests = jnp.sum(jnp.where(slot_at, wanted_rows[:, None], 0), axis=0).reshape(group_size, capacity)
    indices = lax.all_to_all(requests, DP, 0, 0, tiled=True).reshape(-1)

    query_scaled = query_hidden.astype(jnp.float32) * norm_gain
    tool_scaled = tool_hidden.astype(jnp.float32) * norm_gain
    query_squares, tool_squares = lax.psum(
        (jnp.sum(query_scaled * query_scaled, axis=1), jnp.sum(tool_scaled * tool_scaled, axis=1)),
        "section",
    )
    query_norm = jnp.sqrt(query_squares + EPSILON)
    tool_norm = jnp.sqrt(tool_squares + EPSILON)
    query_unit32 = query_scaled / query_norm[:, None]
    tool_unit32 = tool_scaled / tool_norm[:, None]
    query_unit = query_unit32.astype(jnp.bfloat16)
    tool_unit = tool_unit32.astype(jnp.bfloat16)

    tool_ids = jnp.arange(tool_count, dtype=jnp.int32)
    pick_tool = (indices[:, None] == tool_ids[None, :]).astype(jnp.bfloat16)
    answers = jnp.dot(pick_tool, tool_unit, preferred_element_type=jnp.float32).astype(jnp.bfloat16)
    back_unit = lax.all_to_all(
        answers.reshape(group_size, capacity, features), DP, 0, 0, tiled=True
    ).reshape(places, features)

    local_part = lax.dot_general(
        query_unit, tool_unit, (((1,), (1,)), ((), ())), preferred_element_type=jnp.float32
    )
    slot_grid = slot_at.reshape(query_count, per_query, places)
    every_place = lax.dot_general(
        query_unit, back_unit, (((1,), (1,)), ((), ())), preferred_element_type=jnp.float32
    )
    hard_part = jnp.sum(jnp.where(slot_grid, every_place[:, None, :], 0.0), axis=2)
    shard_scores, negative_scores = (
        lax.psum(local_part.astype(jnp.bfloat16), "section").astype(jnp.float32),
        lax.psum(hard_part.astype(jnp.bfloat16), "section").astype(jnp.float32),
    )
    shard_gradients, negative_gradients = softmax_grads(
        shard_scores, negative_scores, positive_tool, hard_valid
    )
    spread_grads = jnp.sum(
        jnp.where(slot_grid, negative_gradients.astype(jnp.float32)[:, :, None], 0.0), axis=1
    ).astype(jnp.bfloat16)

    sent_terms = lax.dot_general(
        spread_grads, query_unit, (((0,), (0,)), ((), ())), preferred_element_type=jnp.float32
    ).astype(jnp.bfloat16)
    arrived_terms = lax.all_to_all(
        sent_terms.reshape(group_size, capacity, features), DP, 0, 0, tiled=True
    ).reshape(places, features)

    query_pull = jnp.dot(shard_gradients, tool_unit, preferred_element_type=jnp.float32)
    query_pull = query_pull + jnp.dot(spread_grads, back_unit, preferred_element_type=jnp.float32)
    tool_pull = lax.dot_general(
        shard_gradients, query_unit, (((0,), (0,)), ((), ())), preferred_element_type=jnp.float32
    )
    tool_pull = tool_pull + lax.dot_general(
        pick_tool, arrived_terms, (((0,), (0,)), ((), ())), preferred_element_type=jnp.float32
    )

    query_inner, tool_inner = lax.psum(
        (jnp.sum(query_unit32 * query_pull, axis=1), jnp.sum(tool_unit32 * tool_pull, axis=1)),
        "section",
    )
    query_back = (query_pull - query_unit32 * query_inner[:, None]) / query_norm[:, None]
    tool_back = (tool_pull - tool_unit32 * tool_inner[:, None]) / tool_norm[:, None]
    query_grad = (query_back * norm_gain).astype(jnp.bfloat16)
    tool_grad = (tool_back * norm_gain).astype(jnp.bfloat16)
    gain_terms = jnp.sum(query_back * query_hidden.astype(jnp.float32), axis=0) + jnp.sum(
        tool_back * tool_hidden.astype(jnp.float32), axis=0
    )
    pair_terms = lax.psum(gain_terms, "dc")
    chips = lax.axis_size(DP[:2])
    everyone = jnp.broadcast_to(pair_terms[None, :], (chips, gain_terms.shape[0]))
    gain_grad = jnp.sum(lax.all_to_all(everyone, DP[:2], 0, 0, tiled=True), axis=0)
    return (query_grad, tool_grad, gain_grad)


def split_dp(mesh):
    dp = mesh.shape["dp"]
    cores = 2 if dp % 2 == 0 else 1
    rest = dp // cores
    ys = 4 if rest % 4 == 0 else 1
    devices = np.asarray(mesh.devices).reshape(rest // ys, ys, cores, mesh.shape["section"])
    return Mesh(devices, DP + ("section",))


def solution(mesh):
    fine = split_dp(mesh)
    return jax.shard_map(
        body,
        mesh=fine,
        in_specs=(
            P(DP, "section"),
            P(DP, "section"),
            P("section"),
            P(DP),
            P(DP, None),
            P(DP, None),
            P(DP, None),
        ),
        out_specs=(P(DP, "section"), P(DP, "section"), P("section")),
        check_vma=False,
    )
```

```python
import jax
import jax.numpy as jnp
import numpy as np
from jax import lax
from jax.sharding import Mesh
from jax.sharding import PartitionSpec as P

EPSILON = 1e-06
SOFTMAX_TEMP = 0.05
DP = ("dz", "dy", "dc")


def softmax_grads(shard_scores, negative_scores, positive, valid_mask):
    selected_rows = lax.broadcasted_iota(jnp.int32, shard_scores.shape, 1) == positive[:, None]
    softmax_weights = jnp.exp(shard_scores / SOFTMAX_TEMP)
    shard_probabilities = softmax_weights / jnp.sum(softmax_weights, axis=1, keepdims=True)
    positive_score = jnp.sum(jnp.where(selected_rows, shard_scores, 0.0), axis=1)
    positive_weight = jnp.exp(positive_score / SOFTMAX_TEMP)
    negative_weights = jnp.where(valid_mask > 0, jnp.exp(negative_scores / SOFTMAX_TEMP), 0.0)
    negative_weight_sum = positive_weight + jnp.sum(negative_weights, axis=1)
    shard_gradients = (
        (
            shard_probabilities
            + jnp.where(selected_rows, (positive_weight / negative_weight_sum - 2.0)[:, None], 0.0)
        )
        / SOFTMAX_TEMP
    ).astype(jnp.bfloat16)
    negative_gradients = (negative_weights / (negative_weight_sum[:, None] * SOFTMAX_TEMP)).astype(
        jnp.bfloat16
    )
    return (shard_gradients, negative_gradients)


def section_sum(value):
    parts = lax.axis_size("section")
    flat = value.reshape(-1)
    gathered = lax.all_to_all(jnp.broadcast_to(flat[None, :], (parts, flat.shape[0])), "section", 0, 0, tiled=True)
    return jnp.sum(gathered.astype(jnp.float32), axis=0).reshape(value.shape)


def body(query_hidden, tool_hidden, norm_gain, positive_tool, hard_owner, hard_row, hard_valid):
    query_count, features = query_hidden.shape
    tool_count = tool_hidden.shape[0]
    per_query = hard_owner.shape[1]
    slots = query_count * per_query
    group_size = lax.axis_size(DP)
    capacity = max(2, 2 * query_count * per_query // group_size)
    places = group_size * capacity

    owners = hard_owner.reshape(-1)
    wanted_rows = hard_row.reshape(-1)
    usable = hard_valid.reshape(-1) > 0
    slot_ids = jnp.arange(slots, dtype=jnp.int32)
    same_earlier = (
        (owners[:, None] == owners[None, :]) & usable[None, :] & (slot_ids[None, :] < slot_ids[:, None])
    )
    slot_place = jnp.sum(same_earlier.astype(jnp.int32), axis=1)
    target = jnp.where(usable, owners * capacity + slot_place, places)
    place_ids = jnp.arange(places, dtype=jnp.int32)
    slot_at = target[:, None] == place_ids[None, :]
    requests = jnp.sum(jnp.where(slot_at, wanted_rows[:, None], 0), axis=0).reshape(group_size, capacity)
    indices = lax.all_to_all(requests, DP, 0, 0, tiled=True).reshape(-1)

    query_scaled = query_hidden.astype(jnp.float32) * norm_gain
    tool_scaled = tool_hidden.astype(jnp.float32) * norm_gain
    query_squares, tool_squares = lax.psum(
        (jnp.sum(query_scaled * query_scaled, axis=1), jnp.sum(tool_scaled * tool_scaled, axis=1)),
        "section",
    )
    query_norm = jnp.sqrt(query_squares + EPSILON)
    tool_norm = jnp.sqrt(tool_squares + EPSILON)
    query_unit32 = query_scaled / query_norm[:, None]
    tool_unit32 = tool_scaled / tool_norm[:, None]
    query_unit = query_unit32.astype(jnp.bfloat16)
    tool_unit = tool_unit32.astype(jnp.bfloat16)

    tool_ids = jnp.arange(tool_count, dtype=jnp.int32)
    pick_tool = (indices[:, None] == tool_ids[None, :]).astype(jnp.bfloat16)
    answers = jnp.dot(pick_tool, tool_unit, preferred_element_type=jnp.float32).astype(jnp.bfloat16)
    back_unit = lax.all_to_all(
        answers.reshape(group_size, capacity, features), DP, 0, 0, tiled=True
    ).reshape(places, features)

    local_part = lax.dot_general(
        query_unit, tool_unit, (((1,), (1,)), ((), ())), preferred_element_type=jnp.float32
    )
    slot_grid = slot_at.reshape(query_count, per_query, places)
    every_place = lax.dot_general(
        query_unit, back_unit, (((1,), (1,)), ((), ())), preferred_element_type=jnp.float32
    )
    hard_part = jnp.sum(jnp.where(slot_grid, every_place[:, None, :], 0.0), axis=2)
    shard_scores, negative_scores = (
        lax.psum(local_part.astype(jnp.bfloat16), "section").astype(jnp.float32),
        section_sum(hard_part.astype(jnp.bfloat16)),
    )
    shard_gradients, negative_gradients = softmax_grads(
        shard_scores, negative_scores, positive_tool, hard_valid
    )
    spread_grads = jnp.sum(
        jnp.where(slot_grid, negative_gradients.astype(jnp.float32)[:, :, None], 0.0), axis=1
    ).astype(jnp.bfloat16)

    sent_terms = lax.dot_general(
        spread_grads, query_unit, (((0,), (0,)), ((), ())), preferred_element_type=jnp.float32
    ).astype(jnp.bfloat16)
    arrived_terms = lax.all_to_all(
        sent_terms.reshape(group_size, capacity, features), DP, 0, 0, tiled=True
    ).reshape(places, features)

    query_pull = jnp.dot(shard_gradients, tool_unit, preferred_element_type=jnp.float32)
    query_pull = query_pull + jnp.dot(spread_grads, back_unit, preferred_element_type=jnp.float32)
    tool_pull = lax.dot_general(
        shard_gradients, query_unit, (((0,), (0,)), ((), ())), preferred_element_type=jnp.float32
    )
    tool_pull = tool_pull + lax.dot_general(
        pick_tool, arrived_terms, (((0,), (0,)), ((), ())), preferred_element_type=jnp.float32
    )

    inner = section_sum(
        jnp.stack([jnp.sum(query_unit32 * query_pull, axis=1), jnp.sum(tool_unit32 * tool_pull, axis=1)])
    )
    query_inner, tool_inner = inner[0], inner[1]
    query_back = (query_pull - query_unit32 * query_inner[:, None]) / query_norm[:, None]
    tool_back = (tool_pull - tool_unit32 * tool_inner[:, None]) / tool_norm[:, None]
    query_grad = (query_back * norm_gain).astype(jnp.bfloat16)
    tool_grad = (tool_back * norm_gain).astype(jnp.bfloat16)
    gain_terms = jnp.sum(query_back * query_hidden.astype(jnp.float32), axis=0) + jnp.sum(
        tool_back * tool_hidden.astype(jnp.float32), axis=0
    )
    pair_terms = lax.psum(gain_terms, "dc")
    chips = lax.axis_size(DP[:2])
    everyone = jnp.broadcast_to(pair_terms[None, :], (chips, gain_terms.shape[0]))
    gain_grad = jnp.sum(lax.all_to_all(everyone, DP[:2], 0, 0, tiled=True), axis=0)
    return (query_grad, tool_grad, gain_grad)


def split_dp(mesh):
    dp = mesh.shape["dp"]
    cores = 2 if dp % 2 == 0 else 1
    rest = dp // cores
    ys = 4 if rest % 4 == 0 else 1
    devices = np.asarray(mesh.devices).reshape(rest // ys, ys, cores, mesh.shape["section"])
    return Mesh(devices, DP + ("section",))


def solution(mesh):
    fine = split_dp(mesh)
    return jax.shard_map(
        body,
        mesh=fine,
        in_specs=(
            P(DP, "section"),
            P(DP, "section"),
            P("section"),
            P(DP),
            P(DP, None),
            P(DP, None),
            P(DP, None),
        ),
        out_specs=(P(DP, "section"), P(DP, "section"), P("section")),
        check_vma=False,
    )
```

```python
import jax
import jax.numpy as jnp
import numpy as np
from jax import lax
from jax.sharding import Mesh
from jax.sharding import PartitionSpec as P

EPSILON = 1e-06
SOFTMAX_TEMP = 0.05
DP = ("dz", "dy", "dc")


def softmax_grads(shard_scores, negative_scores, positive, valid_mask):
    selected_rows = lax.broadcasted_iota(jnp.int32, shard_scores.shape, 1) == positive[:, None]
    softmax_weights = jnp.exp(shard_scores / SOFTMAX_TEMP)
    shard_probabilities = softmax_weights / jnp.sum(softmax_weights, axis=1, keepdims=True)
    positive_score = jnp.sum(jnp.where(selected_rows, shard_scores, 0.0), axis=1)
    positive_weight = jnp.exp(positive_score / SOFTMAX_TEMP)
    negative_weights = jnp.where(valid_mask > 0, jnp.exp(negative_scores / SOFTMAX_TEMP), 0.0)
    negative_weight_sum = positive_weight + jnp.sum(negative_weights, axis=1)
    shard_gradients = (
        (
            shard_probabilities
            + jnp.where(selected_rows, (positive_weight / negative_weight_sum - 2.0)[:, None], 0.0)
        )
        / SOFTMAX_TEMP
    ).astype(jnp.bfloat16)
    negative_gradients = (negative_weights / (negative_weight_sum[:, None] * SOFTMAX_TEMP)).astype(
        jnp.bfloat16
    )
    return (shard_gradients, negative_gradients)


def body(query_hidden, tool_hidden, norm_gain, positive_tool, hard_owner, hard_row, hard_valid):
    query_count, features = query_hidden.shape
    tool_count = tool_hidden.shape[0]
    per_query = hard_owner.shape[1]
    slots = query_count * per_query
    group_size = lax.axis_size(DP)
    capacity = max(2, 2 * query_count * per_query // group_size)
    places = group_size * capacity

    owners = hard_owner.reshape(-1)
    wanted_rows = hard_row.reshape(-1)
    usable = hard_valid.reshape(-1) > 0
    slot_ids = jnp.arange(slots, dtype=jnp.int32)
    same_earlier = (
        (owners[:, None] == owners[None, :]) & usable[None, :] & (slot_ids[None, :] < slot_ids[:, None])
    )
    slot_place = jnp.sum(same_earlier.astype(jnp.int32), axis=1)
    target = jnp.where(usable, owners * capacity + slot_place, places)
    place_ids = jnp.arange(places, dtype=jnp.int32)
    slot_at = target[:, None] == place_ids[None, :]
    requests = jnp.sum(jnp.where(slot_at, wanted_rows[:, None], 0), axis=0).reshape(group_size, capacity)
    indices = lax.all_to_all(requests, DP, 0, 0, tiled=True).reshape(-1)

    query_scaled = query_hidden.astype(jnp.float32) * norm_gain
    tool_scaled = tool_hidden.astype(jnp.float32) * norm_gain
    query_squares, tool_squares = lax.psum(
        (jnp.sum(query_scaled * query_scaled, axis=1), jnp.sum(tool_scaled * tool_scaled, axis=1)),
        "section",
    )
    query_norm = jnp.sqrt(query_squares + EPSILON)
    tool_norm = jnp.sqrt(tool_squares + EPSILON)
    query_unit32 = query_scaled / query_norm[:, None]
    tool_unit32 = tool_scaled / tool_norm[:, None]
    query_unit = query_unit32.astype(jnp.bfloat16)
    tool_unit = tool_unit32.astype(jnp.bfloat16)

    tool_ids = jnp.arange(tool_count, dtype=jnp.int32)
    pick_tool = (indices[:, None] == tool_ids[None, :]).astype(jnp.bfloat16)
    answers = jnp.dot(pick_tool, tool_unit, preferred_element_type=jnp.float32).astype(jnp.bfloat16)
    back_unit = lax.all_to_all(
        answers.reshape(group_size, capacity, features), DP, 0, 0, tiled=True
    ).reshape(places, features)

    local_part = lax.dot_general(
        query_unit, tool_unit, (((1,), (1,)), ((), ())), preferred_element_type=jnp.float32
    )
    slot_grid = slot_at.reshape(query_count, per_query, places)
    every_place = lax.dot_general(
        query_unit, back_unit, (((1,), (1,)), ((), ())), preferred_element_type=jnp.float32
    )
    hard_part = jnp.sum(jnp.where(slot_grid, every_place[:, None, :], 0.0), axis=2)
    shard_scores, negative_scores = (
        lax.psum(local_part.astype(jnp.bfloat16), "section").astype(jnp.float32),
        lax.psum(hard_part.astype(jnp.bfloat16), "section").astype(jnp.float32),
    )
    shard_gradients, negative_gradients = softmax_grads(
        shard_scores, negative_scores, positive_tool, hard_valid
    )
    spread_grads = jnp.sum(
        jnp.where(slot_grid, negative_gradients.astype(jnp.float32)[:, :, None], 0.0), axis=1
    ).astype(jnp.bfloat16)

    sent_terms = lax.dot_general(
        spread_grads, query_unit, (((0,), (0,)), ((), ())), preferred_element_type=jnp.float32
    ).astype(jnp.bfloat16)
    arrived_terms = lax.all_to_all(
        sent_terms.reshape(group_size, capacity, features), DP, 0, 0, tiled=True
    ).reshape(places, features)

    query_pull = jnp.dot(shard_gradients, tool_unit, preferred_element_type=jnp.float32)
    query_pull = query_pull + jnp.dot(spread_grads, back_unit, preferred_element_type=jnp.float32)
    tool_pull = lax.dot_general(
        shard_gradients, query_unit, (((0,), (0,)), ((), ())), preferred_element_type=jnp.float32
    )
    arrived_terms, tool_pull, query_pull = lax.optimization_barrier((arrived_terms, tool_pull, query_pull))
    tool_pull = tool_pull + lax.dot_general(
        pick_tool, arrived_terms, (((0,), (0,)), ((), ())), preferred_element_type=jnp.float32
    )

    query_inner, tool_inner = lax.psum(
        (jnp.sum(query_unit32 * query_pull, axis=1), jnp.sum(tool_unit32 * tool_pull, axis=1)),
        "section",
    )
    query_back = (query_pull - query_unit32 * query_inner[:, None]) / query_norm[:, None]
    tool_back = (tool_pull - tool_unit32 * tool_inner[:, None]) / tool_norm[:, None]
    query_grad = (query_back * norm_gain).astype(jnp.bfloat16)
    tool_grad = (tool_back * norm_gain).astype(jnp.bfloat16)
    gain_terms = jnp.sum(query_back * query_hidden.astype(jnp.float32), axis=0) + jnp.sum(
        tool_back * tool_hidden.astype(jnp.float32), axis=0
    )
    pair_terms = lax.psum(gain_terms, "dc")
    chips = lax.axis_size(DP[:2])
    everyone = jnp.broadcast_to(pair_terms[None, :], (chips, gain_terms.shape[0]))
    gain_grad = jnp.sum(lax.all_to_all(everyone, DP[:2], 0, 0, tiled=True), axis=0)
    return (query_grad, tool_grad, gain_grad)


def split_dp(mesh):
    dp = mesh.shape["dp"]
    cores = 2 if dp % 2 == 0 else 1
    rest = dp // cores
    ys = 4 if rest % 4 == 0 else 1
    devices = np.asarray(mesh.devices).reshape(rest // ys, ys, cores, mesh.shape["section"])
    return Mesh(devices, DP + ("section",))


def solution(mesh):
    fine = split_dp(mesh)
    return jax.shard_map(
        body,
        mesh=fine,
        in_specs=(
            P(DP, "section"),
            P(DP, "section"),
            P("section"),
            P(DP),
            P(DP, None),
            P(DP, None),
            P(DP, None),
        ),
        out_specs=(P(DP, "section"), P(DP, "section"), P("section")),
        check_vma=False,
    )
```

```python
import jax
import jax.numpy as jnp
import numpy as np
from jax import lax
from jax.sharding import Mesh
from jax.sharding import PartitionSpec as P

EPSILON = 1e-06
SOFTMAX_TEMP = 0.05
DP = ("dz", "dy", "dc")


def softmax_grads(shard_scores, negative_scores, positive, valid_mask):
    selected_rows = lax.broadcasted_iota(jnp.int32, shard_scores.shape, 1) == positive[:, None]
    softmax_weights = jnp.exp(shard_scores / SOFTMAX_TEMP)
    shard_probabilities = softmax_weights / jnp.sum(softmax_weights, axis=1, keepdims=True)
    positive_score = jnp.sum(jnp.where(selected_rows, shard_scores, 0.0), axis=1)
    positive_weight = jnp.exp(positive_score / SOFTMAX_TEMP)
    negative_weights = jnp.where(valid_mask > 0, jnp.exp(negative_scores / SOFTMAX_TEMP), 0.0)
    negative_weight_sum = positive_weight + jnp.sum(negative_weights, axis=1)
    shard_gradients = (
        (
            shard_probabilities
            + jnp.where(selected_rows, (positive_weight / negative_weight_sum - 2.0)[:, None], 0.0)
        )
        / SOFTMAX_TEMP
    ).astype(jnp.bfloat16)
    negative_gradients = (negative_weights / (negative_weight_sum[:, None] * SOFTMAX_TEMP)).astype(
        jnp.bfloat16
    )
    return (shard_gradients, negative_gradients)


def section_sum(value):
    parts = lax.axis_size("section")
    flat = value.reshape(-1)
    gathered = lax.all_to_all(jnp.broadcast_to(flat[None, :], (parts, flat.shape[0])), "section", 0, 0, tiled=True)
    return jnp.sum(gathered.astype(jnp.float32), axis=0).reshape(value.shape)


def body(query_hidden, tool_hidden, norm_gain, positive_tool, hard_owner, hard_row, hard_valid):
    query_count, features = query_hidden.shape
    tool_count = tool_hidden.shape[0]
    per_query = hard_owner.shape[1]
    slots = query_count * per_query
    group_size = lax.axis_size(DP)
    capacity = max(2, 2 * query_count * per_query // group_size)
    places = group_size * capacity

    owners = hard_owner.reshape(-1)
    wanted_rows = hard_row.reshape(-1)
    usable = hard_valid.reshape(-1) > 0
    slot_ids = jnp.arange(slots, dtype=jnp.int32)
    same_earlier = (
        (owners[:, None] == owners[None, :]) & usable[None, :] & (slot_ids[None, :] < slot_ids[:, None])
    )
    slot_place = jnp.sum(same_earlier.astype(jnp.int32), axis=1)
    target = jnp.where(usable, owners * capacity + slot_place, places)
    place_ids = jnp.arange(places, dtype=jnp.int32)
    slot_at = target[:, None] == place_ids[None, :]
    requests = jnp.sum(jnp.where(slot_at, wanted_rows[:, None], 0), axis=0).reshape(group_size, capacity)
    indices = lax.all_to_all(requests, DP, 0, 0, tiled=True).reshape(-1)

    query_scaled = query_hidden.astype(jnp.float32) * norm_gain
    tool_scaled = tool_hidden.astype(jnp.float32) * norm_gain
    query_squares, tool_squares = lax.psum(
        (jnp.sum(query_scaled * query_scaled, axis=1), jnp.sum(tool_scaled * tool_scaled, axis=1)),
        "section",
    )
    query_norm = jnp.sqrt(query_squares + EPSILON)
    tool_norm = jnp.sqrt(tool_squares + EPSILON)
    query_unit32 = query_scaled / query_norm[:, None]
    tool_unit32 = tool_scaled / tool_norm[:, None]
    query_unit = query_unit32.astype(jnp.bfloat16)
    tool_unit = tool_unit32.astype(jnp.bfloat16)

    tool_ids = jnp.arange(tool_count, dtype=jnp.int32)
    pick_tool = (indices[:, None] == tool_ids[None, :]).astype(jnp.bfloat16)
    answers = jnp.dot(pick_tool, tool_unit, preferred_element_type=jnp.float32).astype(jnp.bfloat16)
    back_unit = lax.all_to_all(
        answers.reshape(group_size, capacity, features), DP, 0, 0, tiled=True
    ).reshape(places, features)

    local_part = lax.dot_general(
        query_unit, tool_unit, (((1,), (1,)), ((), ())), preferred_element_type=jnp.float32
    )
    slot_grid = slot_at.reshape(query_count, per_query, places)
    every_place = lax.dot_general(
        query_unit, back_unit, (((1,), (1,)), ((), ())), preferred_element_type=jnp.float32
    )
    hard_part = jnp.sum(jnp.where(slot_grid, every_place[:, None, :], 0.0), axis=2)
    shard_scores, negative_scores = (
        lax.psum(local_part.astype(jnp.bfloat16), "section").astype(jnp.float32),
        lax.psum(hard_part.astype(jnp.bfloat16), "section").astype(jnp.float32),
    )
    shard_gradients, negative_gradients = softmax_grads(
        shard_scores, negative_scores, positive_tool, hard_valid
    )
    spread_grads = jnp.sum(
        jnp.where(slot_grid, negative_gradients.astype(jnp.float32)[:, :, None], 0.0), axis=1
    ).astype(jnp.bfloat16)

    sent_terms = lax.dot_general(
        spread_grads, query_unit, (((0,), (0,)), ((), ())), preferred_element_type=jnp.float32
    ).astype(jnp.bfloat16)
    arrived_terms = lax.all_to_all(
        sent_terms.reshape(group_size, capacity, features), DP, 0, 0, tiled=True
    ).reshape(places, features)

    query_pull = jnp.dot(shard_gradients, tool_unit, preferred_element_type=jnp.float32)
    query_pull = query_pull + jnp.dot(spread_grads, back_unit, preferred_element_type=jnp.float32)
    tool_pull = lax.dot_general(
        shard_gradients, query_unit, (((0,), (0,)), ((), ())), preferred_element_type=jnp.float32
    )
    tool_pull = tool_pull + lax.dot_general(
        pick_tool, arrived_terms, (((0,), (0,)), ((), ())), preferred_element_type=jnp.float32
    )

    inner = section_sum(
        jnp.stack([jnp.sum(query_unit32 * query_pull, axis=1), jnp.sum(tool_unit32 * tool_pull, axis=1)])
    )
    query_inner, tool_inner = inner[0], inner[1]
    query_back = (query_pull - query_unit32 * query_inner[:, None]) / query_norm[:, None]
    tool_back = (tool_pull - tool_unit32 * tool_inner[:, None]) / tool_norm[:, None]
    query_grad = (query_back * norm_gain).astype(jnp.bfloat16)
    tool_grad = (tool_back * norm_gain).astype(jnp.bfloat16)
    gain_terms = jnp.sum(query_back * query_hidden.astype(jnp.float32), axis=0) + jnp.sum(
        tool_back * tool_hidden.astype(jnp.float32), axis=0
    )
    pair_terms = lax.psum(gain_terms, "dc")
    chips = lax.axis_size(DP[:2])
    everyone = jnp.broadcast_to(pair_terms[None, :], (chips, gain_terms.shape[0]))
    gain_grad = jnp.sum(lax.all_to_all(everyone, DP[:2], 0, 0, tiled=True), axis=0)
    return (query_grad, tool_grad, gain_grad)


def split_dp(mesh):
    dp = mesh.shape["dp"]
    cores = 2 if dp % 2 == 0 else 1
    rest = dp // cores
    ys = 4 if rest % 4 == 0 else 1
    devices = np.asarray(mesh.devices).reshape(rest // ys, ys, cores, mesh.shape["section"])
    return Mesh(devices, DP + ("section",))


def solution(mesh):
    fine = split_dp(mesh)
    return jax.shard_map(
        body,
        mesh=fine,
        in_specs=(
            P(DP, "section"),
            P(DP, "section"),
            P("section"),
            P(DP),
            P(DP, None),
            P(DP, None),
            P(DP, None),
        ),
        out_specs=(P(DP, "section"), P(DP, "section"), P("section")),
        check_vma=False,
    )
```

```python
import jax
import jax.numpy as jnp
import numpy as np
from jax import lax
from jax.sharding import Mesh
from jax.sharding import PartitionSpec as P

EPSILON = 1e-06
SOFTMAX_TEMP = 0.05
DP = ("dz", "dy", "dc")


def softmax_grads(shard_scores, negative_scores, positive, valid_mask):
    selected_rows = lax.broadcasted_iota(jnp.int32, shard_scores.shape, 1) == positive[:, None]
    softmax_weights = jnp.exp(shard_scores / SOFTMAX_TEMP)
    shard_probabilities = softmax_weights / jnp.sum(softmax_weights, axis=1, keepdims=True)
    positive_score = jnp.sum(jnp.where(selected_rows, shard_scores, 0.0), axis=1)
    positive_weight = jnp.exp(positive_score / SOFTMAX_TEMP)
    negative_weights = jnp.where(valid_mask > 0, jnp.exp(negative_scores / SOFTMAX_TEMP), 0.0)
    negative_weight_sum = positive_weight + jnp.sum(negative_weights, axis=1)
    shard_gradients = (
        (
            shard_probabilities
            + jnp.where(selected_rows, (positive_weight / negative_weight_sum - 2.0)[:, None], 0.0)
        )
        / SOFTMAX_TEMP
    ).astype(jnp.bfloat16)
    negative_gradients = (negative_weights / (negative_weight_sum[:, None] * SOFTMAX_TEMP)).astype(
        jnp.bfloat16
    )
    return (shard_gradients, negative_gradients)


def body(query_hidden, tool_hidden, norm_gain, positive_tool, hard_owner, hard_row, hard_valid):
    query_count, features = query_hidden.shape
    tool_count = tool_hidden.shape[0]
    per_query = hard_owner.shape[1]
    slots = query_count * per_query
    group_size = lax.axis_size(DP)
    capacity = max(2, 2 * query_count * per_query // group_size)
    places = group_size * capacity

    owners = hard_owner.reshape(-1)
    wanted_rows = hard_row.reshape(-1)
    usable = hard_valid.reshape(-1) > 0
    slot_ids = jnp.arange(slots, dtype=jnp.int32)
    same_earlier = (
        (owners[:, None] == owners[None, :]) & usable[None, :] & (slot_ids[None, :] < slot_ids[:, None])
    )
    slot_place = jnp.sum(same_earlier.astype(jnp.int32), axis=1)
    target = jnp.where(usable, owners * capacity + slot_place, places)
    place_ids = jnp.arange(places, dtype=jnp.int32)
    slot_at = target[:, None] == place_ids[None, :]
    requests = jnp.sum(jnp.where(slot_at, wanted_rows[:, None], 0), axis=0).reshape(group_size, capacity)
    indices = lax.all_to_all(requests, DP, 0, 0, tiled=True).reshape(-1)

    query_scaled = query_hidden.astype(jnp.float32) * norm_gain
    tool_scaled = tool_hidden.astype(jnp.float32) * norm_gain
    query_squares, tool_squares = lax.psum(
        (jnp.sum(query_scaled * query_scaled, axis=1), jnp.sum(tool_scaled * tool_scaled, axis=1)),
        "section",
    )
    query_norm = jnp.sqrt(query_squares + EPSILON)
    tool_norm = jnp.sqrt(tool_squares + EPSILON)
    query_unit32 = query_scaled / query_norm[:, None]
    tool_unit32 = tool_scaled / tool_norm[:, None]
    query_unit = query_unit32.astype(jnp.bfloat16)
    tool_unit = tool_unit32.astype(jnp.bfloat16)

    tool_ids = jnp.arange(tool_count, dtype=jnp.int32)
    pick_tool = (indices[:, None] == tool_ids[None, :]).astype(jnp.bfloat16)
    answers = jnp.dot(pick_tool, tool_unit, preferred_element_type=jnp.float32).astype(jnp.bfloat16)
    back_unit = lax.all_to_all(
        answers.reshape(group_size, capacity, features), DP, 0, 0, tiled=True
    ).reshape(places, features)

    slot_of_query = slot_at.reshape(query_count, per_query, places).any(axis=1)
    placed_queries = lax.dot_general(
        slot_of_query.astype(jnp.bfloat16), query_unit, (((0,), (0,)), ((), ())),
        preferred_element_type=jnp.float32,
    ).astype(jnp.bfloat16)
    back_unit, placed_queries = lax.optimization_barrier((back_unit, placed_queries))
    local_part = lax.dot_general(
        query_unit, tool_unit, (((1,), (1,)), ((), ())), preferred_element_type=jnp.float32
    )
    slot_grid = slot_at.reshape(query_count, per_query, places)
    every_place = lax.dot_general(
        query_unit, back_unit, (((1,), (1,)), ((), ())), preferred_element_type=jnp.float32
    )
    hard_part = jnp.sum(jnp.where(slot_grid, every_place[:, None, :], 0.0), axis=2)
    shard_scores, negative_scores = (
        lax.psum(local_part.astype(jnp.bfloat16), "section").astype(jnp.float32),
        lax.psum(hard_part.astype(jnp.bfloat16), "section").astype(jnp.float32),
    )
    shard_gradients, negative_gradients = softmax_grads(
        shard_scores, negative_scores, positive_tool, hard_valid
    )
    spread_grads = jnp.sum(
        jnp.where(slot_grid, negative_gradients.astype(jnp.float32)[:, :, None], 0.0), axis=1
    ).astype(jnp.bfloat16)

    place_grads = jnp.sum(spread_grads.astype(jnp.float32), axis=0)
    sent_terms = (place_grads[:, None] * placed_queries.astype(jnp.float32)).astype(jnp.bfloat16)
    arrived_terms = lax.all_to_all(
        sent_terms.reshape(group_size, capacity, features), DP, 0, 0, tiled=True
    ).reshape(places, features)

    query_pull = jnp.dot(shard_gradients, tool_unit, preferred_element_type=jnp.float32)
    query_pull = query_pull + jnp.dot(spread_grads, back_unit, preferred_element_type=jnp.float32)
    tool_pull = lax.dot_general(
        shard_gradients, query_unit, (((0,), (0,)), ((), ())), preferred_element_type=jnp.float32
    )
    tool_pull = tool_pull + lax.dot_general(
        pick_tool, arrived_terms, (((0,), (0,)), ((), ())), preferred_element_type=jnp.float32
    )

    query_inner, tool_inner = lax.psum(
        (jnp.sum(query_unit32 * query_pull, axis=1), jnp.sum(tool_unit32 * tool_pull, axis=1)),
        "section",
    )
    query_back = (query_pull - query_unit32 * query_inner[:, None]) / query_norm[:, None]
    tool_back = (tool_pull - tool_unit32 * tool_inner[:, None]) / tool_norm[:, None]
    query_grad = (query_back * norm_gain).astype(jnp.bfloat16)
    tool_grad = (tool_back * norm_gain).astype(jnp.bfloat16)
    gain_terms = jnp.sum(query_back * query_hidden.astype(jnp.float32), axis=0) + jnp.sum(
        tool_back * tool_hidden.astype(jnp.float32), axis=0
    )
    pair_terms = lax.psum(gain_terms, "dc")
    chips = lax.axis_size(DP[:2])
    everyone = jnp.broadcast_to(pair_terms[None, :], (chips, gain_terms.shape[0]))
    gain_grad = jnp.sum(lax.all_to_all(everyone, DP[:2], 0, 0, tiled=True), axis=0)
    return (query_grad, tool_grad, gain_grad)


def split_dp(mesh):
    dp = mesh.shape["dp"]
    cores = 2 if dp % 2 == 0 else 1
    rest = dp // cores
    ys = 4 if rest % 4 == 0 else 1
    devices = np.asarray(mesh.devices).reshape(rest // ys, ys, cores, mesh.shape["section"])
    return Mesh(devices, DP + ("section",))


def solution(mesh):
    fine = split_dp(mesh)
    return jax.shard_map(
        body,
        mesh=fine,
        in_specs=(
            P(DP, "section"),
            P(DP, "section"),
            P("section"),
            P(DP),
            P(DP, None),
            P(DP, None),
            P(DP, None),
        ),
        out_specs=(P(DP, "section"), P(DP, "section"), P("section")),
        check_vma=False,
    )
```

```python
import jax
import jax.numpy as jnp
import numpy as np
from jax import lax
from jax.sharding import Mesh
from jax.sharding import PartitionSpec as P

EPSILON = 1e-06
SOFTMAX_TEMP = 0.05
DP = ("dz", "dy", "dc")


def softmax_grads(shard_scores, negative_scores, positive, valid_mask):
    selected_rows = lax.broadcasted_iota(jnp.int32, shard_scores.shape, 1) == positive[:, None]
    softmax_weights = jnp.exp(shard_scores / SOFTMAX_TEMP)
    shard_probabilities = softmax_weights / jnp.sum(softmax_weights, axis=1, keepdims=True)
    positive_score = jnp.sum(jnp.where(selected_rows, shard_scores, 0.0), axis=1)
    positive_weight = jnp.exp(positive_score / SOFTMAX_TEMP)
    negative_weights = jnp.where(valid_mask > 0, jnp.exp(negative_scores / SOFTMAX_TEMP), 0.0)
    negative_weight_sum = positive_weight + jnp.sum(negative_weights, axis=1)
    shard_gradients = (
        (
            shard_probabilities
            + jnp.where(selected_rows, (positive_weight / negative_weight_sum - 2.0)[:, None], 0.0)
        )
        / SOFTMAX_TEMP
    ).astype(jnp.bfloat16)
    negative_gradients = (negative_weights / (negative_weight_sum[:, None] * SOFTMAX_TEMP)).astype(
        jnp.bfloat16
    )
    return (shard_gradients, negative_gradients)


def section_sum(value):
    parts = lax.axis_size("section")
    flat = value.reshape(-1)
    gathered = lax.all_to_all(jnp.broadcast_to(flat[None, :], (parts, flat.shape[0])), "section", 0, 0, tiled=True)
    return jnp.sum(gathered.astype(jnp.float32), axis=0).reshape(value.shape)


def body(query_hidden, tool_hidden, norm_gain, positive_tool, hard_owner, hard_row, hard_valid):
    query_count, features = query_hidden.shape
    tool_count = tool_hidden.shape[0]
    per_query = hard_owner.shape[1]
    slots = query_count * per_query
    group_size = lax.axis_size(DP)
    capacity = max(2, 2 * query_count * per_query // group_size)
    places = group_size * capacity

    owners = hard_owner.reshape(-1)
    wanted_rows = hard_row.reshape(-1)
    usable = hard_valid.reshape(-1) > 0
    slot_ids = jnp.arange(slots, dtype=jnp.int32)
    same_earlier = (
        (owners[:, None] == owners[None, :]) & usable[None, :] & (slot_ids[None, :] < slot_ids[:, None])
    )
    slot_place = jnp.sum(same_earlier.astype(jnp.int32), axis=1)
    target = jnp.where(usable, owners * capacity + slot_place, places)
    place_ids = jnp.arange(places, dtype=jnp.int32)
    slot_at = target[:, None] == place_ids[None, :]
    requests = jnp.sum(jnp.where(slot_at, wanted_rows[:, None], 0), axis=0).reshape(group_size, capacity)
    indices = lax.all_to_all(requests, DP, 0, 0, tiled=True).reshape(-1)

    query_scaled = query_hidden.astype(jnp.float32) * norm_gain
    tool_scaled = tool_hidden.astype(jnp.float32) * norm_gain
    query_squares, tool_squares = lax.psum(
        (jnp.sum(query_scaled * query_scaled, axis=1), jnp.sum(tool_scaled * tool_scaled, axis=1)),
        "section",
    )
    query_norm = jnp.sqrt(query_squares + EPSILON)
    tool_norm = jnp.sqrt(tool_squares + EPSILON)
    query_unit32 = query_scaled / query_norm[:, None]
    tool_unit32 = tool_scaled / tool_norm[:, None]
    query_unit = query_unit32.astype(jnp.bfloat16)
    tool_unit = tool_unit32.astype(jnp.bfloat16)

    tool_ids = jnp.arange(tool_count, dtype=jnp.int32)
    pick_tool = (indices[:, None] == tool_ids[None, :]).astype(jnp.bfloat16)
    answers = jnp.dot(pick_tool, tool_unit, preferred_element_type=jnp.float32).astype(jnp.bfloat16)
    back_unit = lax.all_to_all(
        answers.reshape(group_size, capacity, features), DP, 0, 0, tiled=True
    ).reshape(places, features)

    slot_of_query = slot_at.reshape(query_count, per_query, places).any(axis=1)
    placed_queries = lax.dot_general(
        slot_of_query.astype(jnp.bfloat16), query_unit, (((0,), (0,)), ((), ())),
        preferred_element_type=jnp.float32,
    ).astype(jnp.bfloat16)
    back_unit, placed_queries = lax.optimization_barrier((back_unit, placed_queries))
    local_part = lax.dot_general(
        query_unit, tool_unit, (((1,), (1,)), ((), ())), preferred_element_type=jnp.float32
    )
    slot_grid = slot_at.reshape(query_count, per_query, places)
    every_place = lax.dot_general(
        query_unit, back_unit, (((1,), (1,)), ((), ())), preferred_element_type=jnp.float32
    )
    hard_part = jnp.sum(jnp.where(slot_grid, every_place[:, None, :], 0.0), axis=2)
    shard_scores, negative_scores = (
        lax.psum(local_part.astype(jnp.bfloat16), "section").astype(jnp.float32),
        section_sum(hard_part.astype(jnp.bfloat16)),
    )
    shard_gradients, negative_gradients = softmax_grads(
        shard_scores, negative_scores, positive_tool, hard_valid
    )
    spread_grads = jnp.sum(
        jnp.where(slot_grid, negative_gradients.astype(jnp.float32)[:, :, None], 0.0), axis=1
    ).astype(jnp.bfloat16)

    place_grads = jnp.sum(spread_grads.astype(jnp.float32), axis=0)
    sent_terms = (place_grads[:, None] * placed_queries.astype(jnp.float32)).astype(jnp.bfloat16)
    arrived_terms = lax.all_to_all(
        sent_terms.reshape(group_size, capacity, features), DP, 0, 0, tiled=True
    ).reshape(places, features)

    query_pull = jnp.dot(shard_gradients, tool_unit, preferred_element_type=jnp.float32)
    query_pull = query_pull + jnp.dot(spread_grads, back_unit, preferred_element_type=jnp.float32)
    tool_pull = lax.dot_general(
        shard_gradients, query_unit, (((0,), (0,)), ((), ())), preferred_element_type=jnp.float32
    )
    tool_pull = tool_pull + lax.dot_general(
        pick_tool, arrived_terms, (((0,), (0,)), ((), ())), preferred_element_type=jnp.float32
    )

    query_inner, tool_inner = lax.psum(
        (jnp.sum(query_unit32 * query_pull, axis=1), jnp.sum(tool_unit32 * tool_pull, axis=1)),
        "section",
    )
    query_back = (query_pull - query_unit32 * query_inner[:, None]) / query_norm[:, None]
    tool_back = (tool_pull - tool_unit32 * tool_inner[:, None]) / tool_norm[:, None]
    query_grad = (query_back * norm_gain).astype(jnp.bfloat16)
    tool_grad = (tool_back * norm_gain).astype(jnp.bfloat16)
    gain_terms = jnp.sum(query_back * query_hidden.astype(jnp.float32), axis=0) + jnp.sum(
        tool_back * tool_hidden.astype(jnp.float32), axis=0
    )
    pair_terms = lax.psum(gain_terms, "dc")
    chips = lax.axis_size(DP[:2])
    everyone = jnp.broadcast_to(pair_terms[None, :], (chips, gain_terms.shape[0]))
    gain_grad = jnp.sum(lax.all_to_all(everyone, DP[:2], 0, 0, tiled=True), axis=0)
    return (query_grad, tool_grad, gain_grad)


def split_dp(mesh):
    dp = mesh.shape["dp"]
    cores = 2 if dp % 2 == 0 else 1
    rest = dp // cores
    ys = 4 if rest % 4 == 0 else 1
    devices = np.asarray(mesh.devices).reshape(rest // ys, ys, cores, mesh.shape["section"])
    return Mesh(devices, DP + ("section",))


def solution(mesh):
    fine = split_dp(mesh)
    return jax.shard_map(
        body,
        mesh=fine,
        in_specs=(
            P(DP, "section"),
            P(DP, "section"),
            P("section"),
            P(DP),
            P(DP, None),
            P(DP, None),
            P(DP, None),
        ),
        out_specs=(P(DP, "section"), P(DP, "section"), P("section")),
        check_vma=False,
    )
```

```python
import jax
import jax.numpy as jnp
import numpy as np
from jax import lax
from jax.sharding import Mesh
from jax.sharding import PartitionSpec as P

EPSILON = 1e-06
SOFTMAX_TEMP = 0.05
DP = ("dz", "dy", "dc")


def softmax_grads(shard_scores, negative_scores, positive, valid_mask):
    selected_rows = lax.broadcasted_iota(jnp.int32, shard_scores.shape, 1) == positive[:, None]
    softmax_weights = jnp.exp(shard_scores / SOFTMAX_TEMP)
    shard_probabilities = softmax_weights / jnp.sum(softmax_weights, axis=1, keepdims=True)
    positive_score = jnp.sum(jnp.where(selected_rows, shard_scores, 0.0), axis=1)
    positive_weight = jnp.exp(positive_score / SOFTMAX_TEMP)
    negative_weights = jnp.where(valid_mask > 0, jnp.exp(negative_scores / SOFTMAX_TEMP), 0.0)
    negative_weight_sum = positive_weight + jnp.sum(negative_weights, axis=1)
    shard_gradients = (
        (
            shard_probabilities
            + jnp.where(selected_rows, (positive_weight / negative_weight_sum - 2.0)[:, None], 0.0)
        )
        / SOFTMAX_TEMP
    ).astype(jnp.bfloat16)
    negative_gradients = (negative_weights / (negative_weight_sum[:, None] * SOFTMAX_TEMP)).astype(
        jnp.bfloat16
    )
    return (shard_gradients, negative_gradients)


def body(query_hidden, tool_hidden, norm_gain, positive_tool, hard_owner, hard_row, hard_valid):
    query_count, features = query_hidden.shape
    tool_count = tool_hidden.shape[0]
    per_query = hard_owner.shape[1]
    slots = query_count * per_query
    group_size = lax.axis_size(DP)
    capacity = max(2, 2 * query_count * per_query // group_size)
    places = group_size * capacity

    owners = hard_owner.reshape(-1)
    wanted_rows = hard_row.reshape(-1)
    usable = hard_valid.reshape(-1) > 0
    slot_ids = jnp.arange(slots, dtype=jnp.int32)
    same_earlier = (
        (owners[:, None] == owners[None, :]) & usable[None, :] & (slot_ids[None, :] < slot_ids[:, None])
    )
    slot_place = jnp.sum(same_earlier.astype(jnp.int32), axis=1)
    target = jnp.where(usable, owners * capacity + slot_place, places)
    place_ids = jnp.arange(places, dtype=jnp.int32)
    slot_at = target[:, None] == place_ids[None, :]
    requests = jnp.sum(jnp.where(slot_at, wanted_rows[:, None], 0), axis=0).reshape(group_size, capacity)
    indices = lax.all_to_all(requests, DP, 0, 0, tiled=True).reshape(-1)

    query_scaled = query_hidden.astype(jnp.float32) * norm_gain
    tool_scaled = tool_hidden.astype(jnp.float32) * norm_gain
    query_squares, tool_squares = lax.psum(
        (jnp.sum(query_scaled * query_scaled, axis=1), jnp.sum(tool_scaled * tool_scaled, axis=1)),
        "section",
    )
    query_norm = jnp.sqrt(query_squares + EPSILON)
    tool_norm = jnp.sqrt(tool_squares + EPSILON)
    query_unit32 = query_scaled / query_norm[:, None]
    tool_unit32 = tool_scaled / tool_norm[:, None]
    query_unit = query_unit32.astype(jnp.bfloat16)
    tool_unit = tool_unit32.astype(jnp.bfloat16)

    tool_ids = jnp.arange(tool_count, dtype=jnp.int32)
    pick_tool = (indices[:, None] == tool_ids[None, :]).astype(jnp.bfloat16)
    answers = jnp.dot(pick_tool, tool_unit, preferred_element_type=jnp.float32).astype(jnp.bfloat16)
    back_unit = lax.all_to_all(
        answers.reshape(group_size, capacity, features), DP, 0, 0, tiled=True
    ).reshape(places, features)

    slot_of_query = slot_at.reshape(query_count, per_query, places).any(axis=1)
    placed_queries = lax.dot_general(
        slot_of_query.astype(jnp.bfloat16), query_unit, (((0,), (0,)), ((), ())),
        preferred_element_type=jnp.float32,
    ).astype(jnp.bfloat16)
    back_unit, placed_queries = lax.optimization_barrier((back_unit, placed_queries))
    local_part = lax.dot_general(
        query_unit, tool_unit, (((1,), (1,)), ((), ())), preferred_element_type=jnp.float32
    )
    slot_grid = slot_at.reshape(query_count, per_query, places)
    every_place = lax.dot_general(
        query_unit, back_unit, (((1,), (1,)), ((), ())), preferred_element_type=jnp.float32
    )
    hard_part = jnp.sum(jnp.where(slot_grid, every_place[:, None, :], 0.0), axis=2)
    shard_scores, negative_scores = (
        lax.psum(local_part.astype(jnp.bfloat16), "section").astype(jnp.float32),
        lax.psum(hard_part.astype(jnp.bfloat16), "section").astype(jnp.float32),
    )
    shard_gradients, negative_gradients = softmax_grads(
        shard_scores, negative_scores, positive_tool, hard_valid
    )
    spread_grads = jnp.sum(
        jnp.where(slot_grid, negative_gradients.astype(jnp.float32)[:, :, None], 0.0), axis=1
    ).astype(jnp.bfloat16)

    place_grads = jnp.sum(spread_grads.astype(jnp.float32), axis=0)
    sent_terms = (place_grads[:, None] * placed_queries.astype(jnp.float32)).astype(jnp.bfloat16)
    arrived_terms = lax.all_to_all(
        sent_terms.reshape(group_size, capacity, features), DP, 0, 0, tiled=True
    ).reshape(places, features)

    query_pull = jnp.dot(shard_gradients, tool_unit, preferred_element_type=jnp.float32)
    query_pull = query_pull + jnp.dot(spread_grads, back_unit, preferred_element_type=jnp.float32)
    query_inner = lax.psum(jnp.sum(query_unit32 * query_pull, axis=1), "section")
    query_back = (query_pull - query_unit32 * query_inner[:, None]) / query_norm[:, None]
    query_grad = (query_back * norm_gain).astype(jnp.bfloat16)
    query_gain = jnp.sum(query_back * query_hidden.astype(jnp.float32), axis=0)
    arrived_terms, query_grad, query_gain = lax.optimization_barrier((arrived_terms, query_grad, query_gain))
    tool_pull = lax.dot_general(
        shard_gradients, query_unit, (((0,), (0,)), ((), ())), preferred_element_type=jnp.float32
    )
    tool_pull = tool_pull + lax.dot_general(
        pick_tool, arrived_terms, (((0,), (0,)), ((), ())), preferred_element_type=jnp.float32
    )

    tool_inner = lax.psum(jnp.sum(tool_unit32 * tool_pull, axis=1), "section")
    tool_back = (tool_pull - tool_unit32 * tool_inner[:, None]) / tool_norm[:, None]
    tool_grad = (tool_back * norm_gain).astype(jnp.bfloat16)
    gain_terms = query_gain + jnp.sum(tool_back * tool_hidden.astype(jnp.float32), axis=0)
    pair_terms = lax.psum(gain_terms, "dc")
    chips = lax.axis_size(DP[:2])
    everyone = jnp.broadcast_to(pair_terms[None, :], (chips, gain_terms.shape[0]))
    gain_grad = jnp.sum(lax.all_to_all(everyone, DP[:2], 0, 0, tiled=True), axis=0)
    return (query_grad, tool_grad, gain_grad)


def split_dp(mesh):
    dp = mesh.shape["dp"]
    cores = 2 if dp % 2 == 0 else 1
    rest = dp // cores
    ys = 4 if rest % 4 == 0 else 1
    devices = np.asarray(mesh.devices).reshape(rest // ys, ys, cores, mesh.shape["section"])
    return Mesh(devices, DP + ("section",))


def solution(mesh):
    fine = split_dp(mesh)
    return jax.shard_map(
        body,
        mesh=fine,
        in_specs=(
            P(DP, "section"),
            P(DP, "section"),
            P("section"),
            P(DP),
            P(DP, None),
            P(DP, None),
            P(DP, None),
        ),
        out_specs=(P(DP, "section"), P(DP, "section"), P("section")),
        check_vma=False,
    )
```
